256 devices in a mesh: dp: 2 (over core), blk: 128 (over z, x, y).
Axes of the slice: x: 4, y: 4, z: 8, core: 2. Of those that a mesh axis runs over, the one named last changes fastest.
Arguments:
- features: bfloat16 [2, 65536, 128], P('dp', 'blk'), may hold values from -24 to 24
- tile_mask: int32 [2, 128], P('dp', 'blk'), may hold values 0 or 1
- w_first: bfloat16 [3456, 128], replicated, may hold values from -0.109375 to 0.109375
- w_second: bfloat16 [3456, 128], replicated, may hold values from -0.109375 to 0.109375
- cotangent: bfloat16 [2, 65536, 128], P('dp', 'blk'), may hold values from -6 to 6
Outputs:
- grad_first: float32 [3456, 128], replicated
- grad_second: float32 [3456, 128], replicated
- feature_grad: bfloat16 [2, 65536, 128], P('dp', 'blk')
The draws below stay inside these ranges and needn't reach their ends.
All inputs are finite; a program needn't handle non-finite values. No bound on the sum of `tile_mask` on one device may be relied on, other than what follows from the above.
Results may differ from the reference program's by a relative error of at most 0.0039.
Values may be sent and summed in bfloat16 or wider, within the bound.
A program may use at most 64 MiB of HBM per device.

```python
import jax
import jax.numpy as jnp
from jax import lax

C = 128
TILE = 8
TX = 1
SAMPLES = 2
TILES = 128
CELLS = 65536
N_BLK = 128


def with_ends(entries, rng, smallest, high):
    spot = [jax.random.randint(jax.random.fold_in(rng, axis), (), 0, length) for axis, length in enumerate(entries.shape)]
    widest = entries.shape.index(max(entries.shape))
    neighbour = spot[:widest] + [(spot[widest] + 1) % entries.shape[widest]] + spot[widest + 1:]
    return entries.at[tuple(spot)].set(smallest).at[tuple(neighbour)].set(high)


def raised(values, stream_key, source, target, blocks, factor):
    def block_of(axis_at):
        return (jnp.arange(values.shape[axis_at]) // (values.shape[axis_at] // blocks)).reshape((-1,) + (1,) * (values.ndim - 1 - axis_at))

    one_side = jax.random.permutation(stream_key, blocks)[block_of(target)]
    other_side = (block_of(target) + blocks // 2) % blocks
    return jnp.where((block_of(source) == one_side) | (block_of(source) == other_side), factor * values, values)


def steps_of(stream_key, shape, pieces, smallest, largest):
    def one(dim, blocks):
        steps = jax.random.uniform(jax.random.fold_in(jax.random.fold_in(stream_key, 6), dim), (blocks,), jnp.float32, smallest / len(pieces), largest / len(pieces))
        return jnp.repeat(jnp.exp(steps), shape[dim] // blocks).reshape((-1,) + (1,) * (len(shape) - dim - 1))

    factor_of = one(*pieces[0])
    for cut in pieces[1:]:
        factor_of = factor_of * one(*cut)
    return factor_of


def centred(key, dims, scale, bound, split=(), kind=jnp.bfloat16):
    drawn = scale * jax.random.normal(key, dims, jnp.float32)
    if split:
        drawn = drawn * steps_of(key, dims, split, -0.22, 0.18)
    return jnp.clip(drawn, -bound, bound).astype(kind)


def bell_draw_with(key, shape, scale, limit, cuts, heavy, held_as=jnp.bfloat16):
    values = scale * jax.random.normal(key, shape, jnp.float32)
    if cuts:
        values = values * steps_of(key, shape, cuts, -0.22, 0.18)
    return jnp.clip(raised(values, jax.random.fold_in(key, 3), *heavy), -limit, limit).astype(held_as)


def setup_inputs(seed: int = 0) -> dict:
    keys = jax.random.split(jax.random.key(seed), 6)
    features = bell_draw_with(keys[0], (SAMPLES, CELLS, C), 1.0, 24.0, ((0, 2), (1, 128)), (1, 2, 128, 5.5))
    tile_mask = with_ends((jax.random.randint(keys[1], (SAMPLES, TILES), 0, 4) < 3).astype(jnp.int32), jax.random.fold_in(keys[1], 1), 0, 1)
    w_first = centred(keys[2], (27 * C, C), (27 * C) ** -0.5, 0.109375)
    w_second = centred(keys[3], (27 * C, C), (27 * C) ** -0.5, 0.109375)
    cotangent = centred(keys[4], (SAMPLES, CELLS, C), 1.0, 6.0, ((0, 2), (1, 128)))
    return {"features": features, "tile_mask": tile_mask, "w_first": w_first, "w_second": w_second, "cotangent": cotangent}


unscale = 1.0 / 512.0


def stack_depth(padded, depth_z):
    return jnp.concatenate([padded[:, :, shift_z:shift_z + depth_z, :] for shift_z in range(3)], axis=-1)


def arrange(weight):
    width_in = weight.shape[0] // 27
    width_out = weight.shape[1]
    shaped = weight.reshape(width_in, 3, 3, 3, width_out).transpose(1, 2, 3, 0, 4)
    return shaped.reshape(3, 3, 3 * width_in, width_out)


def arrange_flipped(weight):
    width_in = weight.shape[0] // 27
    width_out = weight.shape[1]
    shaped = weight.reshape(width_in, 3, 3, 3, width_out)[:, ::-1, ::-1, ::-1, :].transpose(1, 2, 3, 4, 0)
    return shaped.reshape(3, 3, 3 * width_out, width_in)


def convolve(padded, kernel):
    size_x = padded.shape[0] - 2
    size_y = padded.shape[1] - 2
    size_z = padded.shape[2] - 2
    stacked = stack_depth(padded, size_z)
    summed = jnp.zeros((size_x * size_y * size_z, kernel.shape[-1]), jnp.float32)
    for step_x in range(3):
        for step_y in range(3):
            slab_rows = stacked[step_x:step_x + size_x, step_y:step_y + size_y].reshape(-1, stacked.shape[-1])
            summed = summed + jnp.dot(slab_rows, kernel[step_x, step_y], preferred_element_type=jnp.float32)
    return summed


def correlate(padded, grads):
    size_x = padded.shape[0] - 2
    size_y = padded.shape[1] - 2
    size_z = padded.shape[2] - 2
    width_in = padded.shape[3]
    width_out = grads.shape[1]
    stacked = stack_depth(padded, size_z)
    blocks = []
    for step_x in range(3):
        for step_y in range(3):
            slab_rows = stacked[step_x:step_x + size_x, step_y:step_y + size_y].reshape(-1, stacked.shape[-1])
            blocks.append(lax.dot_general(slab_rows, grads, (((0,), (0,)), ((), ())), preferred_element_type=jnp.float32))
    joined = jnp.stack(blocks).reshape(3, 3, 3, width_in, width_out).transpose(3, 0, 1, 2, 4)
    return joined.reshape(27 * width_in, width_out)


def to_grid(rows, width):
    shaped = rows.reshape(N_BLK // 16, 4, 4, TX * TILE, TILE, TILE, width).transpose(0, 3, 1, 4, 2, 5, 6)
    return shaped.reshape((N_BLK // 16) * TX * TILE, 4 * TILE, 4 * TILE, width)


def to_rows(grid, width):
    shaped = grid.reshape(N_BLK // 16, TX * TILE, 4, TILE, 4, TILE, width).transpose(0, 2, 4, 1, 3, 5, 6)
    return shaped.reshape(N_BLK * TX * TILE * TILE * TILE, width)


def surround(grid):
    return jnp.pad(grid, ((1, 1), (1, 1), (1, 1), (0, 0)))


def reference(features, tile_mask, w_first, w_second, cotangent):
    kernel_first = arrange(w_first)
    kernel_second_back = arrange_flipped(w_second)
    kernel_first_back = arrange_flipped(w_first)
    width = features.shape[2]
    grad_first = jnp.zeros((27 * width, width), jnp.float32)
    grad_second = jnp.zeros((27 * width, width), jnp.float32)
    results = []
    for sample in range(features.shape[0]):
        keep_rows = jnp.repeat(tile_mask[sample], TILE * TILE * TILE).astype(features.dtype)[:, None]
        grid_shape = to_grid(keep_rows, 1).shape
        keep = to_grid(keep_rows, 1).reshape(-1, 1)
        inputs = to_grid(features[sample] * keep_rows, width)
        grads_out = to_grid(cotangent[sample] * keep_rows, width)
        grads_flat = grads_out.reshape(-1, width)
        pad_in = surround(inputs)
        pre_act = convolve(pad_in, kernel_first)
        hidden = (jax.nn.silu(pre_act) * keep.astype(jnp.float32)).astype(features.dtype)
        hidden_grid = hidden.reshape(grid_shape[:3] + (width,))
        grad_second = grad_second + correlate(surround(hidden_grid), grads_flat) * unscale
        back = convolve(surround(grads_out), kernel_second_back)
        sigma = jax.nn.sigmoid(pre_act)
        pre_grad = (back * sigma * (1.0 + pre_act * (1.0 - sigma)) * keep.astype(jnp.float32)).astype(features.dtype)
        grad_first = grad_first + correlate(pad_in, pre_grad) * unscale
        pre_grid = pre_grad.reshape(grid_shape[:3] + (width,))
        summed = grads_flat.astype(jnp.float32) + convolve(surround(pre_grid), kernel_first_back)
        result = (summed * keep.astype(jnp.float32)).astype(features.dtype)
        results.append(to_rows(result.reshape(grid_shape[:3] + (width,)), width))
    return grad_first, grad_second, jnp.stack(results)
```

```python
import functools

import jax
import jax.numpy as jnp
from jax import lax
from jax.experimental import pallas as pl
from jax.experimental.pallas import tpu as pltpu
from jax.sharding import PartitionSpec as P

T = 8
C = 128
TAPS = 27
K3 = 9 * C
UNSCALE = 1.0 / 512.0
ZS = 24
MESH = pl.DeviceIdType.MESH

DIRS = [
    (i, j, k)
    for i in (-1, 0, 1)
    for j in (-1, 0, 1)
    for k in (-1, 0, 1)
    if (i, j, k) != (0, 0, 0)
]
DIRS.sort(key=lambda d: -sum(abs(v) for v in d))
SIZES = [T if sum(abs(v) for v in d) == 1 else 1 for d in DIRS]
OFFS = [sum(SIZES[:n]) for n in range(len(DIRS))]
TILES = sum(SIZES)
INDEX = {d: n for n, d in enumerate(DIRS)}


def opposite(d):
    return (-d[0], -d[1], -d[2])


def boundary_tiles(d, halo):
    def at(v):
        if halo:
            return 0 if v < 0 else T + 1
        return 1 if v < 0 else T

    dx, dy, dz = d
    xs = range(1, T + 1) if dx == 0 else [at(dx)]
    ys = range(1, T + 1) if dy == 0 else [at(dy)]
    row = lambda x, y, z: (x * (T + 2) + y) * ZS + z + 7
    if dz == 0:
        return [(row(x, y, 1), 1, T) for x in xs for y in ys]
    z = at(dz)
    if dy == 0:
        return [(row(x, 1, z), ZS, T) for x in xs]
    if dx == 0:
        return [(row(1, ys[0], z), (T + 2) * ZS, T)]
    return [(row(xs[0], ys[0], z), 1, 1)]


def rows_of(start, stride, size):
    return pl.ds(start, size) if stride == 1 else pl.ds(start, size, stride=stride)


class Plan:
    def __init__(self, nz, nx, ny):
        self.nz, self.nx, self.ny = nz, nx, ny
        self.n1 = nx
        self.r1 = 64 // nx
        self.t2 = -(-TAPS // ny)
        self.t3 = -(-self.t2 // nz)
        self.slots = self.t3 * nz


def kernel(
    plan,
    mask_ref, feat_hbm, cot_hbm, w1_hbm, w2_hbm,
    fg_ref, g1_ref, g2_ref,
    feat, cot, w1, w2, wf, w1r, w2r, b1,
    pad_i, pad_g, pad_p, st_i, st_g, st_p,
    send_a, recv_a, send_b, recv_b,
    in_t, hid_t, pg_own,
    grads, r0, s1_send, s1_recv, s1_buf, s2_send, s2_recv, s2_buf, s3_recv, ag,
    load_sem, ha_send, ha_recv, hb_send, hb_recv, red_send, red_recv,
):
    nz, nx, ny = plan.nz, plan.nx, plan.ny
    n1, n2, r1, t2, t3 = nx, ny, plan.r1, plan.t2, plan.t3
    core = lax.axis_index("dp")
    blk = lax.axis_index("blk")
    cz = blk // (nx * ny)
    cx = (blk // ny) % nx
    cy = blk % ny

    loads = [
        pltpu.make_async_copy(src, dst, load_sem.at[n])
        for n, (src, dst) in enumerate(((feat_hbm, feat), (cot_hbm, cot), (w1_hbm, w1), (w2_hbm, w2)))
    ]
    for copy in loads:
        copy.start()

    recv_a[...] = jnp.zeros_like(recv_a)
    recv_b[...] = jnp.zeros_like(recv_b)

    step1 = ny - (ny - 1) * core
    step2 = 1 + (ny - 1) * core
    c1 = cx + (cy - cx) * core
    c2 = cy + (cx - cy) * core
    base1 = blk - c1 * step1
    base2 = blk - c2 * step2
    plane = blk - cz * (nx * ny)

    def peer1(k):
        return (core, base1 + (c1 + k) % n1 * step1)

    def peer2(k):
        return (core, base2 + (c2 + k) % n2 * step2)

    def peerz(k):
        return (core, plane + (cz + k) % nz * (nx * ny))

    partner = (1 - core, blk)

    def valid(d):
        inside = None
        for place, count, v in ((cz, nz, d[0]), (cx, nx, d[1]), (cy, ny, d[2])):
            if v == 0:
                continue
            test = place < count - 1 if v > 0 else place > 0
            inside = test if inside is None else jnp.logical_and(inside, test)
        return inside

    def neighbour(d):
        return (core, blk + d[0] * (nx * ny) + d[1] * ny + d[2])

    barrier = pltpu.get_barrier_semaphore()
    count = jnp.int32(1 + (n1 - 1) + (n2 - 1) + (nz - 1))
    peers = [partner] + [peer1(k) for k in range(1, n1)] + [peer2(k) for k in range(1, n2)]
    peers += [peerz(k) for k in range(1, nz)]
    for peer in peers:
        pl.semaphore_signal(barrier, inc=1, device_id=peer, device_id_type=MESH)
    for d in DIRS:
        if sum(abs(v) for v in d) > 1:
            here = valid(d)
            count = count + here.astype(jnp.int32)

            @pl.when(here)
            def _():
                pl.semaphore_signal(barrier, inc=1, device_id=neighbour(d), device_id_type=MESH)

    keep = mask_ref[0, 0].astype(jnp.float32)

    def fill_own(pad, values):
        pad3 = pad.reshape((T + 2) * (T + 2), ZS, C)
        for x in range(T):
            pad3[(x + 1) * (T + 2) + 1:(x + 1) * (T + 2) + 1 + T, 8:16, :] = (
                values[x * 64:(x + 1) * 64].reshape(T, T, C)
            )

    def stage(d, pad, send, base):
        for n, (start, stride, size) in enumerate(boundary_tiles(d, False)):
            send[base + n, 0:size] = pad[rows_of(start, stride, size), :].astype(jnp.bfloat16)

    def fill_halo(d, pad, recv, base):
        for n, (start, stride, size) in enumerate(boundary_tiles(d, True)):
            pad[rows_of(start, stride, size), :] = recv[base + n, 0:size].astype(jnp.float32)

    def halo_copy(d, send, recv, send_sem, recv_sem, arrays):
        there = opposite(d)
        size = SIZES[INDEX[d]] * arrays
        return pltpu.make_async_remote_copy(
            src_ref=send.at[pl.ds(OFFS[INDEX[d]] * arrays, size)],
            dst_ref=recv.at[pl.ds(OFFS[INDEX[there]] * arrays, size)],
            send_sem=send_sem.at[INDEX[d]],
            recv_sem=recv_sem.at[INDEX[there]],
            device_id=neighbour(d),
            device_id_type=MESH,
        )

    def halo_start(*args):
        for d in DIRS:
            @pl.when(valid(d))
            def _():
                halo_copy(d, *args).start()

    def halo_wait(*args):
        for d in DIRS:
            @pl.when(valid(d))
            def _():
                halo_copy(opposite(d), *args).wait_recv()

    def halo_sent(*args):
        for d in DIRS:
            @pl.when(valid(d))
            def _():
                halo_copy(d, *args).wait_send()

    def build(pad, stacked, reverse):
        pad3 = pad.reshape((T + 2) * (T + 2), ZS, C)

        def body(x, carry):
            for c in range(3):
                shift_z = 2 - c if reverse else c
                column = pad3[pl.ds(x * (T + 2), T + 2), 7 + shift_z:15 + shift_z, :]
                for b in range(3):
                    shift_y = 2 - b if reverse else b
                    lanes = (3 * b + c) * C
                    stacked[x, :, lanes:lanes + C] = (
                        column[shift_y:shift_y + T].reshape(64, C).astype(jnp.bfloat16)
                    )
            return carry

        lax.fori_loop(0, T + 2, body, 0)

    def slab(stacked, a):
        return stacked[a:a + T].reshape(512, K3)

    loads[0].wait()
    loads[1].wait()
    inputs = feat[...].astype(jnp.float32) * keep
    grads_out = cot[...].astype(jnp.float32) * keep
    fill_own(pad_i, inputs)
    fill_own(pad_g, grads_out)
    for d in DIRS:
        size = SIZES[INDEX[d]]
        stage(d, pad_i, send_a, OFFS[INDEX[d]] * 2)
        stage(d, pad_g, send_a, OFFS[INDEX[d]] * 2 + size)
    pl.semaphore_wait(barrier, count)
    args_a = (send_a, recv_a, ha_send, ha_recv, 2)
    halo_start(*args_a)

    in_t[...] = inputs.T.astype(jnp.bfloat16)
    loads[2].wait()
    loads[3].wait()
    for w, arranged, stacked in ((w1, w1r, b1), (w2, w2r, None)):
        wf[...] = w[...].astype(jnp.float32)

        def arrange(n, carry):
            row = pl.multiple_of(n * 16, 16)
            for tap in range(TAPS):
                part = wf[pl.ds(n * (16 * TAPS) + tap, 16, stride=TAPS), :].astype(jnp.bfloat16)
                arranged[pl.ds(row, 16), tap * C:(tap + 1) * C] = part
                if stacked is not None:
                    stacked[pl.ds(pl.multiple_of(tap * C + n * 16, 16), 16), :] = part
            return carry

        lax.fori_loop(0, C // 16, arrange, 0)

    halo_wait(*args_a)
    for d in DIRS:
        size = SIZES[INDEX[d]]
        fill_halo(d, pad_i, recv_a, OFFS[INDEX[d]] * 2)
        fill_halo(d, pad_g, recv_a, OFFS[INDEX[d]] * 2 + size)
    build(pad_i, st_i, False)
    build(pad_g, st_g, True)

    def conv_back(stacked, weight):
        total = None
        for a in range(3):
            term = lax.dot_general(
                slab(stacked, 2 - a), weight[:, a * K3:(a + 1) * K3],
                (((1,), (1,)), ((), ())), preferred_element_type=jnp.float32,
            )
            total = term if total is None else total + term
        return total

    def corr(lhs_t, stacked, out):
        for a in range(3):
            out[:, a * K3:(a + 1) * K3] = jnp.dot(
                lhs_t[...], slab(stacked, 2 - a), preferred_element_type=jnp.float32
            )

    pre_act = None
    for a in range(3):
        term = jnp.dot(slab(st_i, a), b1[a * K3:(a + 1) * K3, :], preferred_element_type=jnp.float32)
        pre_act = term if pre_act is None else pre_act + term
    back = conv_back(st_g, w2r)
    sigma = 1.0 / (1.0 + jnp.exp(-pre_act))
    hid_t[...] = (pre_act * sigma * keep).T.astype(jnp.bfloat16)
    pre_grad = back * sigma * (1.0 + pre_act * (1.0 - sigma)) * keep
    fill_own(pad_p, pre_grad)
    for d in DIRS:
        stage(d, pad_p, send_b, OFFS[INDEX[d]])
    args_b = (send_b, recv_b, hb_send, hb_recv, 1)
    halo_start(*args_b)

    def remote(src, dst, g, n, peer):
        return pltpu.make_async_remote_copy(
            src_ref=src, dst_ref=dst, send_sem=red_send.at[g, n], recv_sem=red_recv.at[g, n],
            device_id=peer, device_id_type=MESH,
        )

    S0, S1 = 0, 1
    S2 = S1 + n1 - 1
    S3 = S2 + n2 - 1
    A3 = S3 + nz - 1
    A2 = A3 + nz - 1
    A1 = A2 + n2 - 1
    A0 = A1 + n1 - 1
    mine = pl.multiple_of(core * 64, 64)
    other = pl.multiple_of(64 - core * 64, 64)

    def pair_copy(g):
        return remote(grads.at[g, pl.ds(other, 64)], r0.at[g], g, S0, partner)

    def s1_copy(g, k):
        return remote(s1_send.at[g, k - 1], s1_recv.at[g, k - 1], g, S1 + k - 1, peer1(k))

    def s2_copy(g, k):
        return remote(s2_send.at[g, k - 1], s2_recv.at[g, k - 1], g, S2 + k - 1, peer2(k))

    def s3_copy(g, k):
        return remote(s2_buf.at[g, (cz + k) % nz], s3_recv.at[g, k - 1], g, S3 + k - 1, peerz(k))

    def a3_copy(g, k, wait):
        at = (cz + (nz - k)) % nz if wait else cz
        ref = ag.at[g, core, c1, c2, pl.ds(at * t3, t3)]
        return remote(ref, ref, g, A3 + k - 1, peerz(k))

    def a2_copy(g, k, wait):
        at = (c2 + (n2 - k)) % n2 if wait else c2
        ref = ag.at[g, core, c1, at, pl.ds(0, t2)]
        return remote(ref, ref, g, A2 + k - 1, peer2(k))

    def a1_copy(g, k, wait):
        at = (c1 + (n1 - k)) % n1 if wait else c1
        ref = ag.at[g, core, at, :, pl.ds(0, t2)]
        return remote(ref, ref, g, A1 + k - 1, peer1(k))

    def a0_copy(g, wait):
        ref = ag.at[g, 1 - core if wait else core, :, :, pl.ds(0, t2)]
        return remote(ref, ref, g, A0, partner)

    def chip_rows(g, j):
        here = pl.multiple_of(j * r1, r1)
        return grads[g, pl.ds(mine + here, r1), :] + r0[g, pl.ds(here, r1), :]

    def scatter1(g):
        pair_copy(g).wait_recv()
        for k in range(1, n1):
            s1_send[g, k - 1] = chip_rows(g, (c1 + k) % n1).astype(jnp.bfloat16)
            s1_copy(g, k).start()

    def scatter2(g):
        total = chip_rows(g, c1)
        for k in range(1, n1):
            s1_copy(g, k).wait_recv()
            total = total + s1_recv[g, k - 1].astype(jnp.float32)
        for j in range(n2):
            for t in range(t2):
                tap = j * t2 + t
                if tap < TAPS:
                    s1_buf[g, j, t] = total[:, tap * C:(tap + 1) * C]
                else:
                    s1_buf[g, j, t] = jnp.zeros((r1, C), jnp.float32)
        for k in range(1, n2):
            s2_send[g, k - 1] = s1_buf[g, (c2 + k) % n2].astype(jnp.bfloat16)
            s2_copy(g, k).start()

    def scatter3(g):
        total = s1_buf[g, c2]
        for k in range(1, n2):
            s2_copy(g, k).wait_recv()
            total = total + s2_recv[g, k - 1].astype(jnp.float32)
        for t in range(plan.slots):
            part = total[t] if t < t2 else jnp.zeros((r1, C), jnp.float32)
            s2_buf[g, t // t3, t % t3] = part
        for k in range(1, nz):
            s3_copy(g, k).start()

    def gather3(g):
        total = s2_buf[g, cz]
        for k in range(1, nz):
            s3_copy(g, k).wait_recv()
            total = total + s3_recv[g, k - 1]
        ag[g, core, c1, c2, pl.ds(cz * t3, t3)] = (total * UNSCALE).astype(jnp.bfloat16)
        for k in range(1, nz):
            a3_copy(g, k, False).start()

    def gather2(g):
        for k in range(1, nz):
            a3_copy(g, k, True).wait_recv()
        for k in range(1, n2):
            a2_copy(g, k, False).start()

    def gather1(g):
        for k in range(1, n2):
            a2_copy(g, k, True).wait_recv()
        for k in range(1, n1):
            a1_copy(g, k, False).start()

    def gather0(g):
        for k in range(1, n1):
            a1_copy(g, k, True).wait_recv()
        a0_copy(g, False).start()

    def unpack(g, half, out):
        def body(n, carry):
            first = (half * 64 + n * r1) * TAPS
            for tap in range(TAPS):
                out[pl.ds(first + tap, r1, stride=TAPS), :] = (
                    ag[g, half, n, tap // t2, tap % t2].astype(jnp.float32)
                )
            return carry

        lax.fori_loop(0, n1, body, 0)

    corr(hid_t, st_g, grads.at[0])
    pair_copy(0).start()
    halo_wait(*args_b)
    for d in DIRS:
        fill_halo(d, pad_p, recv_b, OFFS[INDEX[d]])
    build(pad_p, st_p, True)
    scatter1(0)
    corr(in_t, st_p, grads.at[1])
    pair_copy(1).start()
    scatter2(0)
    scatter1(1)
    result = conv_back(st_p, w1r)
    fg_ref[...] = ((cot[...].astype(jnp.float32) * keep + result) * keep).astype(jnp.bfloat16)
    scatter3(0)
    scatter2(1)
    gather3(0)
    scatter3(1)
    gather2(0)
    gather3(1)
    gather1(0)
    gather2(1)
    gather0(0)
    gather1(1)
    unpack(0, core, g2_ref)
    gather0(1)
    a0_copy(0, True).wait_recv()
    unpack(0, 1 - core, g2_ref)
    unpack(1, core, g1_ref)
    a0_copy(1, True).wait_recv()
    unpack(1, 1 - core, g1_ref)

    halo_sent(*args_a)
    halo_sent(*args_b)
    for g in range(2):
        pair_copy(g).wait_send()
        for k in range(1, n1):
            s1_copy(g, k).wait_send()
            a1_copy(g, k, False).wait_send()
        for k in range(1, n2):
            s2_copy(g, k).wait_send()
            a2_copy(g, k, False).wait_send()
        for k in range(1, nz):
            s3_copy(g, k).wait_send()
            a3_copy(g, k, False).wait_send()
        a0_copy(g, False).wait_send()


def on_device(plan, features, tile_mask, w_first, w_second, cotangent):
    n1, n2, nz, r1, t2, t3 = plan.nx, plan.ny, plan.nz, plan.r1, plan.t2, plan.t3
    f32, bf16 = jnp.float32, jnp.bfloat16
    rows = TAPS * C
    copies = 2 * (n1 - 1 + n2 - 1 + nz - 1 + 1)
    pad = pltpu.VMEM(((T + 2) * (T + 2) * ZS, C), f32)
    stacked = pltpu.VMEM((T + 2, 64, K3), bf16)
    halo_a = pltpu.VMEM((2 * TILES, 8, C), bf16)
    halo_b = pltpu.VMEM((TILES, 8, C), bf16)
    dma = pltpu.SemaphoreType.DMA
    any_spec = pl.BlockSpec(memory_space=pl.ANY)
    vmem_spec = pl.BlockSpec(memory_space=pltpu.VMEM)
    scratch = [
        pltpu.VMEM((512, C), bf16), pltpu.VMEM((512, C), bf16),
        pltpu.VMEM((rows, C), bf16), pltpu.VMEM((rows, C), bf16), pltpu.VMEM((rows, C), f32),
        pltpu.VMEM((C, rows), bf16), pltpu.VMEM((C, rows), bf16), pltpu.VMEM((rows, C), bf16),
        pad, pad, pad, stacked, stacked, stacked,
        halo_a, halo_a, halo_b, halo_b,
        pltpu.VMEM((C, 512), bf16), pltpu.VMEM((C, 512), bf16), pltpu.VMEM((8, C), f32),
        pltpu.VMEM((2, C, rows), f32), pltpu.VMEM((2, 64, rows), f32),
        pltpu.VMEM((2, n1 - 1, r1, rows), bf16), pltpu.VMEM((2, n1 - 1, r1, rows), bf16),
        pltpu.VMEM((2, n2, t2, r1, C), f32),
        pltpu.VMEM((2, n2 - 1, t2, r1, C), bf16), pltpu.VMEM((2, n2 - 1, t2, r1, C), bf16),
        pltpu.VMEM((2, nz, t3, r1, C), f32), pltpu.VMEM((2, nz - 1, t3, r1, C), f32),
        pltpu.VMEM((2, 2, n1, n2, plan.slots, r1, C), bf16),
        dma((4,)), dma((26,)), dma((26,)), dma((26,)), dma((26,)),
        dma((2, copies)), dma((2, copies)),
    ]
    feature_grad, grad_first, grad_second = pl.pallas_call(
        functools.partial(kernel, plan),
        out_shape=(
            jax.ShapeDtypeStruct((512, C), bf16),
            jax.ShapeDtypeStruct((rows, C), f32),
            jax.ShapeDtypeStruct((rows, C), f32),
        ),
        in_specs=[pl.BlockSpec(memory_space=pltpu.SMEM)] + [any_spec] * 4,
        out_specs=(vmem_spec,) * 3,
        scratch_shapes=scratch,
        compiler_params=pltpu.CompilerParams(collective_id=0, has_side_effects=True),
        name="block_backward",
    )(tile_mask, features[0], cotangent[0], w_first, w_second)
    return grad_first, grad_second, feature_grad[None]


def solution(mesh):
    blocks = mesh.shape["blk"]
    ny = nx = 4 if blocks >= 16 else 2
    plan = Plan(blocks // (nx * ny), nx, ny)
    in_specs = (P("dp", "blk", None), P("dp", "blk"), P(), P(), P("dp", "blk", None))
    out_specs = (P(), P(), P("dp", "blk", None))
    return jax.shard_map(
        functools.partial(on_device, plan), mesh=mesh, in_specs=in_specs, out_specs=out_specs, check_vma=False
    )
```

```python
import functools

import jax
import jax.numpy as jnp
from jax import lax
from jax.experimental import pallas as pl
from jax.experimental.pallas import tpu as pltpu
from jax.sharding import PartitionSpec as P

T = 8
C = 128
TAPS = 27
K3 = 9 * C
UNSCALE = 1.0 / 512.0
ZS = 24
MESH = pl.DeviceIdType.MESH

DIRS = [
    (i, j, k)
    for i in (-1, 0, 1)
    for j in (-1, 0, 1)
    for k in (-1, 0, 1)
    if (i, j, k) != (0, 0, 0)
]
DIRS.sort(key=lambda d: -sum(abs(v) for v in d))
SIZES = [T if sum(abs(v) for v in d) == 1 else 1 for d in DIRS]
OFFS = [sum(SIZES[:n]) for n in range(len(DIRS))]
TILES = sum(SIZES)
INDEX = {d: n for n, d in enumerate(DIRS)}


def opposite(d):
    return (-d[0], -d[1], -d[2])


def boundary_tiles(d, halo):
    def at(v):
        if halo:
            return 0 if v < 0 else T + 1
        return 1 if v < 0 else T

    dx, dy, dz = d
    xs = range(1, T + 1) if dx == 0 else [at(dx)]
    ys = range(1, T + 1) if dy == 0 else [at(dy)]
    row = lambda x, y, z: (x * (T + 2) + y) * ZS + z + 7
    if dz == 0:
        return [(row(x, y, 1), 1, T) for x in xs for y in ys]
    z = at(dz)
    if dy == 0:
        return [(row(x, 1, z), ZS, T) for x in xs]
    if dx == 0:
        return [(row(1, ys[0], z), (T + 2) * ZS, T)]
    return [(row(xs[0], ys[0], z), 1, 1)]


def rows_of(start, stride, size):
    return pl.ds(start, size) if stride == 1 else pl.ds(start, size, stride=stride)


class Plan:
    def __init__(self, nz, nx, ny):
        self.nz, self.nx, self.ny = nz, nx, ny
        self.n1 = nx
        self.r1 = 64 // nx
        self.t2 = -(-TAPS // ny)


def kernel(
    plan,
    mask_ref, feat_hbm, cot_hbm, w1_hbm, w2_hbm,
    fg_ref, ag_out,
    feat, cot, w1, w2, wf, w1r, w2r, b1,
    pad_i, pad_g, pad_p, st_i, st_g, st_p,
    send_a, recv_a, send_b, recv_b,
    pg_t, hid_t,
    grads, r0, s1_send, s1_recv, s1_own, s2_send, s2_recv, z_all, ag,
    load_sem, ha_send, ha_recv, hb_send, hb_recv, red_send, red_recv,
):
    nz, nx, ny = plan.nz, plan.nx, plan.ny
    n1, n2, r1, t2 = nx, ny, plan.r1, plan.t2
    core = lax.axis_index("dp")
    blk = lax.axis_index("blk")
    cz = blk // (nx * ny)
    cx = (blk // ny) % nx
    cy = blk % ny

    loads = [
        pltpu.make_async_copy(src, dst, load_sem.at[n])
        for n, (src, dst) in enumerate(((feat_hbm, feat), (cot_hbm, cot), (w1_hbm, w1), (w2_hbm, w2)))
    ]
    for copy in loads:
        copy.start()

    recv_a[...] = jnp.zeros_like(recv_a)
    recv_b[...] = jnp.zeros_like(recv_b)

    step1 = ny - (ny - 1) * core
    step2 = 1 + (ny - 1) * core
    c1 = cx + (cy - cx) * core
    c2 = cy + (cx - cy) * core
    base1 = blk - c1 * step1
    base2 = blk - c2 * step2
    plane = blk - cz * (nx * ny)

    def peer1(k):
        return (core, base1 + (c1 + k) % n1 * step1)

    def peer2(k):
        return (core, base2 + (c2 + k) % n2 * step2)

    def peerz(k):
        return (core, plane + (cz + k) % nz * (nx * ny))

    partner = (1 - core, blk)

    def valid(d):
        inside = None
        for place, count, v in ((cz, nz, d[0]), (cx, nx, d[1]), (cy, ny, d[2])):
            if v == 0:
                continue
            test = place < count - 1 if v > 0 else place > 0
            inside = test if inside is None else jnp.logical_and(inside, test)
        return inside

    def neighbour(d):
        return (core, blk + d[0] * (nx * ny) + d[1] * ny + d[2])

    barrier = pltpu.get_barrier_semaphore()
    count = jnp.int32(1 + (n1 - 1) + (n2 - 1) + (nz - 1))
    peers = [partner] + [peer1(k) for k in range(1, n1)] + [peer2(k) for k in range(1, n2)]
    peers += [peerz(k) for k in range(1, nz)]
    for peer in peers:
        pl.semaphore_signal(barrier, inc=1, device_id=peer, device_id_type=MESH)
    for d in DIRS:
        if sum(abs(v) for v in d) > 1:
            here = valid(d)
            count = count + here.astype(jnp.int32)

            @pl.when(here)
            def _():
                pl.semaphore_signal(barrier, inc=1, device_id=neighbour(d), device_id_type=MESH)

    keep = mask_ref[0, 0].astype(jnp.float32)

    def fill_own(pad, values):
        pad3 = pad.reshape((T + 2) * (T + 2), ZS, C)
        for x in range(T):
            pad3[(x + 1) * (T + 2) + 1:(x + 1) * (T + 2) + 1 + T, 8:16, :] = (
                values[x * 64:(x + 1) * 64].reshape(T, T, C)
            )

    def stage(d, pad, send, base):
        for n, (start, stride, size) in enumerate(boundary_tiles(d, False)):
            send[base + n, 0:size] = pad[rows_of(start, stride, size), :].astype(jnp.bfloat16)

    def fill_halo(d, pad, recv, base):
        for n, (start, stride, size) in enumerate(boundary_tiles(d, True)):
            pad[rows_of(start, stride, size), :] = recv[base + n, 0:size].astype(jnp.float32)

    def halo_copy(d, send, recv, send_sem, recv_sem, arrays):
        there = opposite(d)
        size = SIZES[INDEX[d]] * arrays
        return pltpu.make_async_remote_copy(
            src_ref=send.at[pl.ds(OFFS[INDEX[d]] * arrays, size)],
            dst_ref=recv.at[pl.ds(OFFS[INDEX[there]] * arrays, size)],
            send_sem=send_sem.at[INDEX[d]],
            recv_sem=recv_sem.at[INDEX[there]],
            device_id=neighbour(d),
            device_id_type=MESH,
        )

    def halo_start(*args):
        for d in DIRS:
            @pl.when(valid(d))
            def _():
                halo_copy(d, *args).start()

    def halo_wait(*args):
        for d in DIRS:
            @pl.when(valid(d))
            def _():
                halo_copy(opposite(d), *args).wait_recv()

    def halo_sent(*args):
        for d in DIRS:
            @pl.when(valid(d))
            def _():
                halo_copy(d, *args).wait_send()

    def build(pad, stacked, reverse):
        pad3 = pad.reshape((T + 2) * (T + 2), ZS, C)

        def body(x, carry):
            for c in range(3):
                shift_z = 2 - c if reverse else c
                column = pad3[pl.ds(x * (T + 2), T + 2), 7 + shift_z:15 + shift_z, :]
                for b in range(3):
                    shift_y = 2 - b if reverse else b
                    lanes = (3 * b + c) * C
                    stacked[x, :, lanes:lanes + C] = (
                        column[shift_y:shift_y + T].reshape(64, C).astype(jnp.bfloat16)
                    )
            return carry

        lax.fori_loop(0, T + 2, body, 0)

    def slab(stacked, a):
        return stacked[a:a + T].reshape(512, K3)

    loads[0].wait()
    loads[1].wait()
    inputs = feat[...].astype(jnp.float32) * keep
    grads_out = cot[...].astype(jnp.float32) * keep
    fill_own(pad_i, inputs)
    fill_own(pad_g, grads_out)
    for d in DIRS:
        size = SIZES[INDEX[d]]
        stage(d, pad_i, send_a, OFFS[INDEX[d]] * 2)
        stage(d, pad_g, send_a, OFFS[INDEX[d]] * 2 + size)
    pl.semaphore_wait(barrier, count)
    args_a = (send_a, recv_a, ha_send, ha_recv, 2)
    halo_start(*args_a)

    for g in range(2):
        grads[g, n2 - 1, :, (TAPS - (n2 - 1) * t2) * C:] = jnp.zeros((C, (n2 * t2 - TAPS) * C), jnp.float32)
    loads[2].wait()
    loads[3].wait()
    for w, arranged, stacked in ((w1, w1r, b1), (w2, w2r, None)):
        wf[...] = w[...].astype(jnp.float32)

        def arrange(n, carry):
            row = pl.multiple_of(n * 16, 16)
            for tap in range(TAPS):
                part = wf[pl.ds(n * (16 * TAPS) + tap, 16, stride=TAPS), :].astype(jnp.bfloat16)
                arranged[pl.ds(row, 16), tap * C:(tap + 1) * C] = part
                if stacked is not None:
                    stacked[pl.ds(pl.multiple_of(tap * C + n * 16, 16), 16), :] = part
            return carry

        lax.fori_loop(0, C // 16, arrange, 0)

    halo_wait(*args_a)
    for d in DIRS:
        size = SIZES[INDEX[d]]
        fill_halo(d, pad_i, recv_a, OFFS[INDEX[d]] * 2)
        fill_halo(d, pad_g, recv_a, OFFS[INDEX[d]] * 2 + size)
    build(pad_i, st_i, False)
    build(pad_g, st_g, True)

    def conv_back(stacked, weight):
        total = None
        for a in range(3):
            term = lax.dot_general(
                slab(stacked, 2 - a), weight[:, a * K3:(a + 1) * K3],
                (((1,), (1,)), ((), ())), preferred_element_type=jnp.float32,
            )
            total = term if total is None else total + term
        return total

    pre_act = None
    for a in range(3):
        term = jnp.dot(slab(st_i, a), b1[a * K3:(a + 1) * K3, :], preferred_element_type=jnp.float32)
        pre_act = term if pre_act is None else pre_act + term
    back = conv_back(st_g, w2r)
    sigma = 1.0 / (1.0 + jnp.exp(-pre_act))
    hid_t[...] = (pre_act * sigma * keep).T.astype(jnp.bfloat16)
    pre_grad = back * sigma * (1.0 + pre_act * (1.0 - sigma)) * keep
    fill_own(pad_p, pre_grad)
    pg_t[...] = pre_grad.T.astype(jnp.bfloat16)

    names = dict(pair=n2, s1=3 * n2, s2=n2 - 1, zs=nz - 1, a2=n2 - 1, a1=3 * n2, a0=n1)
    first_of = {}
    total_sems = 0
    for name, size in names.items():
        first_of[name] = total_sems
        total_sems += size
    started = []

    def remote(src, dst, g, name, n, peer):
        at = first_of[name] + n
        return pltpu.make_async_remote_copy(
            src_ref=src, dst_ref=dst, send_sem=red_send.at[g, at], recv_sem=red_recv.at[g, at],
            device_id=peer, device_id_type=MESH,
        )

    def go(copy):
        copy.start()
        started.append(copy)

    mine = pl.multiple_of(core * 64, 64)
    other = pl.multiple_of(64 - core * 64, 64)
    firsts = ((c2, c1), (c1, c2))
    hop1 = (peer2, peer1)
    hop2 = (peer1, peer2)

    def chunk(g, i):
        return (firsts[g][1] + 1 + i) % n2

    def pair_copy(g, j):
        return remote(grads.at[g, j, pl.ds(other, 64)], r0.at[g, j], g, "pair", j, partner)

    def chip(g, j, block):
        here = pl.multiple_of(block % n1 * r1, r1)
        return grads[g, j, pl.ds(mine + here, r1), :] + r0[g, j, pl.ds(here, r1), :]

    def s1_copy(g, i, k):
        return remote(s1_send.at[g, i, k - 1], s1_recv.at[g, i, k - 1], g, "s1", 3 * i + k - 1, hop1[g](k))

    def s2_copy(g, k):
        return remote(s2_send.at[g, k - 1], s2_recv.at[g, k - 1], g, "s2", k - 1, hop2[g](k))

    def z_copy(g, k, wait):
        ref = z_all.at[g, (cz + (nz - k)) % nz if wait else cz]
        return remote(ref, ref, g, "zs", k - 1, peerz(k))

    def a2_copy(g, k, wait):
        b, j = firsts[g]
        ref = ag.at[g, core, b, (j + (n2 - k)) % n2 if wait else j]
        return remote(ref, ref, g, "a2", k - 1, hop2[g](k))

    def a1_copy(g, m, k, wait):
        b, j = firsts[g]
        ref = ag.at[g, core, (b + (n1 - k)) % n1 if wait else b, (j + (n2 - m)) % n2]
        return remote(ref, ref, g, "a1", 3 * m + k - 1, hop1[g](k))

    def a0_copy(g, n, wait):
        ref = ag.at[g, 1 - core if wait else core, (firsts[g][1 if wait else 0] + (n1 - n)) % n1]
        return remote(ref, ref, g, "a0", n, partner)

    def corr(g, lhs_t, slab_of):
        sent = 0
        for a in range(3):
            part = jnp.dot(lhs_t[...], slab_of(a), preferred_element_type=jnp.float32)
            for n in range(9):
                tap = 9 * a + n
                at = tap % t2 * C
                grads[g, tap // t2, :, at:at + C] = part[:, n * C:(n + 1) * C]
            while sent < n2 and min((sent + 1) * t2, TAPS) <= 9 * (a + 1):
                go(pair_copy(g, sent))
                sent += 1

    far_first = (2, 1, 3)

    def scatter1(g):
        for i in range(n2):
            j = chunk(g, i)
            pair_copy(g, j).wait_recv()
            for k in far_first:
                s1_send[g, i, k - 1] = chip(g, j, firsts[g][0] + k).astype(jnp.bfloat16)
                go(s1_copy(g, i, k))

    def scatter2(g):
        for i in range(n2):
            total = chip(g, chunk(g, i), firsts[g][0])
            for k in range(1, n1):
                s1_copy(g, i, k).wait_recv()
                total = total + s1_recv[g, i, k - 1].astype(jnp.float32)
            if i < n2 - 1:
                s2_send[g, i] = total
                go(s2_copy(g, i + 1))
            else:
                s1_own[g] = total

    z_order = (4, 3, 5, 2, 6, 1, 7)

    def scatter3(g):
        total = s1_own[g]
        for k in range(1, n2):
            s2_copy(g, k).wait_recv()
            total = total + s2_recv[g, k - 1]
        z_all[g, cz] = total.astype(jnp.bfloat16)
        for k in z_order:
            go(z_copy(g, k, False))

    def gather2(g):
        for k in reversed(z_order):
            z_copy(g, k, True).wait_recv()
        total = z_all[g, 0].astype(jnp.float32)
        for z in range(1, nz):
            total = total + z_all[g, z].astype(jnp.float32)
        b, j = firsts[g]
        ag[g, core, b, j] = (total * UNSCALE).astype(jnp.bfloat16)
        for k in far_first:
            go(a2_copy(g, k, False))
        for k in far_first:
            go(a1_copy(g, 0, k, False))

    def gather1(g):
        for m in (1, 3, 2):
            a2_copy(g, m, True).wait_recv()
            for k in far_first:
                go(a1_copy(g, m, k, False))
        go(a0_copy(g, 0, False))

    def gather0(g):
        for k in (1, 3, 2):
            for m in (0, 1, 3, 2):
                a1_copy(g, m, k, True).wait_recv()
            go(a0_copy(g, k, False))

    def finish(g):
        for n in (0, 1, 3, 2):
            a0_copy(g, n, True).wait_recv()
        done = pltpu.make_async_copy(ag.at[g], ag_out.at[g], load_sem.at[4 + g])
        done.start()
        return done

    corr(1, pg_t, lambda a: slab(st_i, a))
    corr(0, hid_t, lambda a: slab(st_g, 2 - a))
    scatter1(1)
    scatter1(0)
    for d in DIRS:
        stage(d, pad_p, send_b, OFFS[INDEX[d]])
    args_b = (send_b, recv_b, hb_send, hb_recv, 1)
    halo_start(*args_b)
    scatter2(1)
    scatter2(0)
    halo_wait(*args_b)
    for d in DIRS:
        fill_halo(d, pad_p, recv_b, OFFS[INDEX[d]])
    build(pad_p, st_p, True)
    scatter3(1)
    scatter3(0)
    result = conv_back(st_p, w1r)
    fg_ref[...] = ((cot[...].astype(jnp.float32) * keep + result) * keep).astype(jnp.bfloat16)
    gather2(1)
    gather2(0)
    gather1(1)
    gather1(0)
    gather0(1)
    gather0(0)
    done1 = finish(1)
    done0 = finish(0)

    halo_sent(*args_a)
    halo_sent(*args_b)
    for copy in started:
        copy.wait_send()
    done1.wait()
    done0.wait()


def unpack_kernel(plan, ag_hbm, fg_hbm, g1_hbm, g2_hbm, fg_out, ag, fg, g1, g2, sems):
    n1, r1, t2 = plan.nx, plan.r1, plan.t2
    rows = r1 * TAPS
    loads = [
        pltpu.make_async_copy(src, dst, sems.at[n])
        for n, (src, dst) in enumerate(((ag_hbm.at[0], ag.at[0]), (ag_hbm.at[1], ag.at[1]), (fg_hbm, fg)))
    ]
    for copy in loads:
        copy.start()
    stores = []

    def put(src, dst):
        copy = pltpu.make_async_copy(src, dst, sems.at[3 + len(stores)])
        copy.start()
        stores.append(copy)

    loads[0].wait()
    for half in range(2):
        for block in range(n1):
            first = (half * n1 + block) * rows
            for tap in range(TAPS):
                lanes = pl.ds(tap % t2 * C, C)
                g2[pl.ds(first + tap, r1, stride=TAPS), :] = (
                    ag[0, half, block, tap // t2, :, lanes].astype(jnp.float32)
                )
            put(g2.at[pl.ds(first, rows)], g2_hbm.at[pl.ds(first, rows)])
    loads[2].wait()
    put(fg, fg_out)
    loads[1].wait()
    for tap in range(TAPS):
        block = ag[1, :, :, tap // t2, :, pl.ds(tap % t2 * C, C)].reshape(C, C)
        g1[pl.ds(tap, C, stride=TAPS), :] = block.astype(jnp.float32).T
    put(g1, g1_hbm)
    for copy in stores:
        copy.wait()


def on_device(plan, features, tile_mask, w_first, w_second, cotangent):
    n1, n2, nz, r1, t2 = plan.nx, plan.ny, plan.nz, plan.r1, plan.t2
    f32, bf16 = jnp.float32, jnp.bfloat16
    rows = TAPS * C
    copies = 7 * n2 + n1 + 2 * (n2 - 1) + nz - 1
    gathered = (2, 2, n1, n2, r1, t2 * C)
    s1_buf = pltpu.VMEM((2, n2, n1 - 1, r1, t2 * C), bf16)
    s2_buf = pltpu.VMEM((2, n2 - 1, r1, t2 * C), f32)
    pad = pltpu.VMEM(((T + 2) * (T + 2) * ZS, C), f32)
    stacked = pltpu.VMEM((T + 2, 64, K3), bf16)
    halo_a = pltpu.VMEM((2 * TILES, 8, C), bf16)
    halo_b = pltpu.VMEM((TILES, 8, C), bf16)
    dma = pltpu.SemaphoreType.DMA
    any_spec = pl.BlockSpec(memory_space=pl.ANY)
    vmem_spec = pl.BlockSpec(memory_space=pltpu.VMEM)
    scratch = [
        pltpu.VMEM((512, C), bf16), pltpu.VMEM((512, C), bf16),
        pltpu.VMEM((rows, C), bf16), pltpu.VMEM((rows, C), bf16), pltpu.VMEM((rows, C), f32),
        pltpu.VMEM((C, rows), bf16), pltpu.VMEM((C, rows), bf16), pltpu.VMEM((rows, C), bf16),
        pad, pad, pad, stacked, stacked, stacked,
        halo_a, halo_a, halo_b, halo_b,
        pltpu.VMEM((C, 512), bf16), pltpu.VMEM((C, 512), bf16),
        pltpu.VMEM((2, n2, C, t2 * C), f32), pltpu.VMEM((2, n2, 64, t2 * C), f32),
        s1_buf, s1_buf, pltpu.VMEM((2, r1, t2 * C), f32), s2_buf, s2_buf,
        pltpu.VMEM((2, nz, r1, t2 * C), bf16),
        pltpu.VMEM(gathered, bf16),
        dma((6,)), dma((26,)), dma((26,)), dma((26,)), dma((26,)),
        dma((2, copies)), dma((2, copies)),
    ]
    partial_fg, partial_ag = pl.pallas_call(
        functools.partial(kernel, plan),
        out_shape=(jax.ShapeDtypeStruct((512, C), bf16), jax.ShapeDtypeStruct(gathered, bf16)),
        in_specs=[pl.BlockSpec(memory_space=pltpu.SMEM)] + [any_spec] * 4,
        out_specs=(vmem_spec, any_spec),
        scratch_shapes=scratch,
        compiler_params=pltpu.CompilerParams(collective_id=0, has_side_effects=True),
        name="block_backward",
    )(tile_mask, features[0], cotangent[0], w_first, w_second)
    grad_first, grad_second, feature_grad = pl.pallas_call(
        functools.partial(unpack_kernel, plan),
        out_shape=(
            jax.ShapeDtypeStruct((rows, C), f32),
            jax.ShapeDtypeStruct((rows, C), f32),
            jax.ShapeDtypeStruct((512, C), bf16),
        ),
        in_specs=[any_spec] * 2,
        out_specs=(any_spec,) * 3,
        scratch_shapes=[
            pltpu.VMEM(gathered, bf16), pltpu.VMEM((512, C), bf16),
            pltpu.VMEM((rows, C), f32), pltpu.VMEM((rows, C), f32), dma((3 + 2 * n1 + 2,)),
        ],
        name="unpack",
    )(partial_ag, partial_fg)
    return grad_first, grad_second, feature_grad[None]


def solution(mesh):
    blocks = mesh.shape["blk"]
    ny = nx = 4 if blocks >= 16 else 2
    plan = Plan(blocks // (nx * ny), nx, ny)
    in_specs = (P("dp", "blk", None), P("dp", "blk"), P(), P(), P("dp", "blk", None))
    out_specs = (P(), P(), P("dp", "blk", None))
    return jax.shard_map(
        functools.partial(on_device, plan), mesh=mesh, in_specs=in_specs, out_specs=out_specs, check_vma=False
    )
```

```python
import functools

import jax
import jax.numpy as jnp
from jax import lax
from jax.experimental import pallas as pl
from jax.experimental.pallas import tpu as pltpu
from jax.sharding import PartitionSpec as P

T = 8
C = 128
TAPS = 27
K3 = 9 * C
UNSCALE = 1.0 / 512.0
ZS = 24
MESH = pl.DeviceIdType.MESH

DIRS = [
    (i, j, k)
    for i in (-1, 0, 1)
    for j in (-1, 0, 1)
    for k in (-1, 0, 1)
    if (i, j, k) != (0, 0, 0)
]
DIRS.sort(key=lambda d: -sum(abs(v) for v in d))
SIZES = [T if sum(abs(v) for v in d) == 1 else 1 for d in DIRS]
OFFS = [sum(SIZES[:n]) for n in range(len(DIRS))]
TILES = sum(SIZES)
INDEX = {d: n for n, d in enumerate(DIRS)}


def opposite(d):
    return (-d[0], -d[1], -d[2])


def boundary_tiles(d, halo):
    def at(v):
        if halo:
            return 0 if v < 0 else T + 1
        return 1 if v < 0 else T

    dx, dy, dz = d
    xs = range(1, T + 1) if dx == 0 else [at(dx)]
    ys = range(1, T + 1) if dy == 0 else [at(dy)]
    row = lambda x, y, z: (x * (T + 2) + y) * ZS + z + 7
    if dz == 0:
        return [(row(x, y, 1), 1, T) for x in xs for y in ys]
    z = at(dz)
    if dy == 0:
        return [(row(x, 1, z), ZS, T) for x in xs]
    if dx == 0:
        return [(row(1, ys[0], z), (T + 2) * ZS, T)]
    return [(row(xs[0], ys[0], z), 1, 1)]


def rows_of(start, stride, size):
    return pl.ds(start, size) if stride == 1 else pl.ds(start, size, stride=stride)


class Plan:
    def __init__(self, nz, nx, ny):
        self.nz, self.nx, self.ny = nz, nx, ny
        self.n1 = nx
        self.r1 = 64 // nx
        self.t2 = -(-TAPS // ny)


def kernel(
    plan,
    mask_ref, feat_hbm, cot_hbm, w1_hbm, w2_hbm,
    fg_out, ag_out,
    feat, cot, w1, w2, wf, w1r, w2r, b1,
    pad_i, pad_g, pad_p, st_i, st_g, st_p,
    send_a, recv_a, send_b, recv_b,
    pg_t, hid_t,
    grads, r0, s1_send, s1_recv, s1_own, s2_send, s2_recv, z_all, ag, fg,
    load_sem, out_sem, ha_sems, hb_sems, red_send, red_recv,
):
    nz, nx, ny = plan.nz, plan.nx, plan.ny
    n1, n2, r1, t2 = nx, ny, plan.r1, plan.t2
    core = lax.axis_index("dp")
    blk = lax.axis_index("blk")
    cz = blk // (nx * ny)
    cx = (blk // ny) % nx
    cy = blk % ny

    loads = [
        pltpu.make_async_copy(src, dst, load_sem.at[n])
        for n, (src, dst) in enumerate(((feat_hbm, feat), (cot_hbm, cot), (w1_hbm, w1), (w2_hbm, w2)))
    ]
    for copy in loads:
        copy.start()

    step1 = ny - (ny - 1) * core
    step2 = 1 + (ny - 1) * core
    c1 = cx + (cy - cx) * core
    c2 = cy + (cx - cy) * core
    base1 = blk - c1 * step1
    base2 = blk - c2 * step2
    plane = blk - cz * (nx * ny)

    def peer1(k):
        return (core, base1 + (c1 + k) % n1 * step1)

    def peer2(k):
        return (core, base2 + (c2 + k) % n2 * step2)

    def peerz(k):
        return (core, plane + (cz + k) % nz * (nx * ny))

    partner = (1 - core, blk)

    def valid(d):
        inside = None
        for place, count, v in ((cz, nz, d[0]), (cx, nx, d[1]), (cy, ny, d[2])):
            if v == 0:
                continue
            test = place < count - 1 if v > 0 else place > 0
            inside = test if inside is None else jnp.logical_and(inside, test)
        return inside

    inside = {d: valid(d).astype(jnp.int32) for d in DIRS}

    def target(d):
        here = inside[d]
        step = d[0] * (nx * ny) + d[1] * ny + d[2]
        return (core + (1 - here) * (1 - 2 * core), blk + here * step)

    barrier = pltpu.get_barrier_semaphore()
    peers = [target(d) for d in DIRS if sum(abs(v) for v in d) > 1]
    peers += [peerz(k) for k in range(1, nz)] + [partner]
    peers += [peer1(k) for k in range(1, n1)] + [peer2(k) for k in range(1, n2)]
    for peer in peers:
        pl.semaphore_signal(barrier, inc=1, device_id=peer, device_id_type=MESH)
    count = len(peers)

    keep = mask_ref[0, 0].astype(jnp.float32)

    def fill_own(pad, values):
        pad3 = pad.reshape((T + 2) * (T + 2), ZS, C)
        for x in range(T):
            pad3[(x + 1) * (T + 2) + 1:(x + 1) * (T + 2) + 1 + T, 8:16, :] = (
                values[x * 64:(x + 1) * 64].reshape(T, T, C)
            )

    def stage(d, pad, send, base):
        for n, (start, stride, size) in enumerate(boundary_tiles(d, False)):
            send[base + n, 0:size] = pad[rows_of(start, stride, size), :].astype(jnp.bfloat16)

    def fill_halo(d, pad, recv, base):
        for n, (start, stride, size) in enumerate(boundary_tiles(d, True)):
            tile = recv[base + n, 0:size].astype(jnp.float32)
            pad[rows_of(start, stride, size), :] = jnp.where(inside[d] > 0, tile, jnp.zeros_like(tile))

    def halo_start(send, recv, sems, arrays):
        for d in DIRS:
            here, there = OFFS[INDEX[d]] * arrays, OFFS[INDEX[opposite(d)]] * arrays
            size = SIZES[INDEX[d]] * arrays
            pltpu.make_async_remote_copy(
                src_ref=send.at[pl.ds(here, size)],
                dst_ref=recv.at[pl.ds(here + inside[d] * (there - here), size)],
                send_sem=sems.at[0], recv_sem=sems.at[1], device_id=target(d), device_id_type=MESH,
            ).start()

    def halo_all(send, recv, sems, arrays):
        return pltpu.make_async_remote_copy(
            src_ref=send, dst_ref=recv, send_sem=sems.at[0], recv_sem=sems.at[1],
            device_id=partner, device_id_type=MESH,
        )

    def halo_wait(*args):
        halo_all(*args).wait_recv()

    def halo_sent(*args):
        halo_all(*args).wait_send()

    def build(pad, stacked, reverse):
        pad3 = pad.reshape((T + 2) * (T + 2), ZS, C)

        def body(x, carry):
            for c in range(3):
                shift_z = 2 - c if reverse else c
                column = pad3[pl.ds(x * (T + 2), T + 2), 7 + shift_z:15 + shift_z, :]
                for b in range(3):
                    shift_y = 2 - b if reverse else b
                    lanes = (3 * b + c) * C
                    stacked[x, :, lanes:lanes + C] = (
                        column[shift_y:shift_y + T].reshape(64, C).astype(jnp.bfloat16)
                    )
            return carry

        lax.fori_loop(0, T + 2, body, 0)

    def slab(stacked, a):
        return stacked[a:a + T].reshape(512, K3)

    loads[0].wait()
    loads[1].wait()
    inputs = feat[...].astype(jnp.float32) * keep
    grads_out = cot[...].astype(jnp.float32) * keep
    fill_own(pad_i, inputs)
    fill_own(pad_g, grads_out)
    for d in DIRS:
        size = SIZES[INDEX[d]]
        stage(d, pad_i, send_a, OFFS[INDEX[d]] * 2)
        stage(d, pad_g, send_a, OFFS[INDEX[d]] * 2 + size)
    pl.semaphore_wait(barrier, count)
    args_a = (send_a, recv_a, ha_sems, 2)
    halo_start(*args_a)

    for g in range(2):
        grads[g, n2 - 1, :, (TAPS - (n2 - 1) * t2) * C:] = jnp.zeros((C, (n2 * t2 - TAPS) * C), jnp.float32)
    loads[2].wait()
    loads[3].wait()
    for w, arranged, stacked in ((w1, w1r, b1), (w2, w2r, None)):
        wf[...] = w[...].astype(jnp.float32)

        def arrange(n, carry):
            row = pl.multiple_of(n * 16, 16)
            for tap in range(TAPS):
                part = wf[pl.ds(n * (16 * TAPS) + tap, 16, stride=TAPS), :].astype(jnp.bfloat16)
                arranged[pl.ds(row, 16), tap * C:(tap + 1) * C] = part
                if stacked is not None:
                    stacked[pl.ds(pl.multiple_of(tap * C + n * 16, 16), 16), :] = part
            return carry

        lax.fori_loop(0, C // 16, arrange, 0)

    halo_wait(*args_a)
    for d in DIRS:
        size = SIZES[INDEX[d]]
        fill_halo(d, pad_i, recv_a, OFFS[INDEX[d]] * 2)
        fill_halo(d, pad_g, recv_a, OFFS[INDEX[d]] * 2 + size)
    build(pad_i, st_i, False)
    build(pad_g, st_g, True)

    def conv_back(stacked, weight):
        total = None
        for a in range(3):
            term = lax.dot_general(
                slab(stacked, 2 - a), weight[:, a * K3:(a + 1) * K3],
                (((1,), (1,)), ((), ())), preferred_element_type=jnp.float32,
            )
            total = term if total is None else total + term
        return total

    recv_first = dict(pair=0, s1=n2, s2=2 * n2, zs=2 * n2 + 1, a2=2 * n2 + 2, a1=3 * n2 + 1, a0=3 * n2 + n1)
    send_index = {name: n for n, name in enumerate(recv_first)}

    def remote(src, dst, g, name, n, peer):
        return pltpu.make_async_remote_copy(
            src_ref=src, dst_ref=dst,
            send_sem=red_send.at[g, send_index[name]], recv_sem=red_recv.at[g, recv_first[name] + n],
            device_id=peer, device_id_type=MESH,
        )

    def arrived(ref, g, name, n=0):
        remote(ref, ref, g, name, n, partner).wait_recv()

    def sent(ref, g, name):
        remote(ref, ref, g, name, 0, partner).wait_send()

    def go(copy):
        copy.start()

    mine = pl.multiple_of(core * 64, 64)
    other = pl.multiple_of(64 - core * 64, 64)
    firsts = ((c2, c1), (c1, c2))
    hop1 = (peer2, peer1)
    hop2 = (peer1, peer2)

    def chunk(g, i):
        own = firsts[g][1]
        return own if i == n2 - 1 else i + (i >= own).astype(jnp.int32)

    def pair_copy(g, j):
        return remote(grads.at[g, j, pl.ds(other, 64)], r0.at[g, j], g, "pair", j, partner)

    def chip(g, j, block):
        here = pl.multiple_of(block % n1 * r1, r1)
        return grads[g, j, pl.ds(mine + here, r1), :] + r0[g, j, pl.ds(here, r1), :]

    def s1_copy(g, i, k):
        return remote(s1_send.at[g, i, k - 1], s1_recv.at[g, i, k - 1], g, "s1", i, hop1[g](k))

    def s2_copy(g, i):
        k = (chunk(g, i) - firsts[g][1] + n2) % n2
        return remote(s2_send.at[g, i], s2_recv.at[g, k - 1], g, "s2", 0, hop2[g](k))

    def z_copy(g, k):
        ref = z_all.at[g, cz]
        return remote(ref, ref, g, "zs", 0, peerz(k))

    def a2_copy(g, k, wait):
        b, j = firsts[g]
        ref = ag.at[g, core, b, (j + (n2 - k)) % n2 if wait else j]
        return remote(ref, ref, g, "a2", k - 1, hop2[g](k))

    def a1_copy(g, m, k):
        b, j = firsts[g]
        ref = ag.at[g, core, b, (j + (n2 - m)) % n2]
        return remote(ref, ref, g, "a1", k - 1, hop1[g](k))

    def a0_copy(g, n, wait):
        ref = ag.at[g, 1 - core if wait else core, (firsts[g][1 if wait else 0] + (n1 - n)) % n1]
        return remote(ref, ref, g, "a0", n, partner)

    def corr(g, lhs_t, slab_of):
        sent = 0
        for a in range(3):
            part = jnp.dot(lhs_t[...], slab_of(a), preferred_element_type=jnp.float32)
            for n in range(9):
                tap = 9 * a + n
                at = tap % t2 * C
                grads[g, tap // t2, :, at:at + C] = part[:, n * C:(n + 1) * C]
            while sent < n2 and min((sent + 1) * t2, TAPS) <= 9 * (a + 1):
                go(pair_copy(g, sent))
                sent += 1

    far_first = (2, 1, 3)

    def scatter1(g):
        for i in range(n2):
            j = chunk(g, i)
            pair_copy(g, j).wait_recv()
            for k in far_first:
                s1_send[g, i, k - 1] = chip(g, j, firsts[g][0] + k).astype(jnp.bfloat16)
                go(s1_copy(g, i, k))

    def scatter2(g):
        for i in range(n2):
            total = chip(g, chunk(g, i), firsts[g][0])
            arrived(s1_recv.at[g, i], g, "s1", i)
            for k in range(1, n1):
                total = total + s1_recv[g, i, k - 1].astype(jnp.float32)
            if i < n2 - 1:
                s2_send[g, i] = total
                go(s2_copy(g, i))
            else:
                s1_own[g] = total

    z_order = (4, 3, 5, 2, 6, 1, 7)

    def scatter3(g):
        total = s1_own[g]
        arrived(s2_recv.at[g], g, "s2")
        for k in range(1, n2):
            total = total + s2_recv[g, k - 1]
        z_all[g, cz] = total.astype(jnp.bfloat16)
        for k in z_order:
            go(z_copy(g, k))

    def gather2(g):
        arrived(z_all.at[g, pl.ds(0, nz - 1)], g, "zs")
        total = z_all[g, 0].astype(jnp.float32)
        for z in range(1, nz):
            total = total + z_all[g, z].astype(jnp.float32)
        b, j = firsts[g]
        ag[g, core, b, j] = (total * UNSCALE).astype(jnp.bfloat16)
        for k in far_first:
            go(a2_copy(g, k, False))
        for k in far_first:
            go(a1_copy(g, 0, k))

    def gather1(g):
        for m in (1, 3, 2):
            a2_copy(g, m, True).wait_recv()
            for k in far_first:
                go(a1_copy(g, m, k))
        go(a0_copy(g, 0, False))
        put(g, core, firsts[g][0])

    def gather0(g):
        for k in (1, 3, 2):
            block = (firsts[g][0] + (n1 - k)) % n1
            arrived(ag.at[g, core, block], g, "a1", k - 1)
            go(a0_copy(g, k, False))
            put(g, core, block)

    def put(g, half, block):
        copy = pltpu.make_async_copy(ag.at[g, half, block], ag_out.at[g, half, block], out_sem.at[0])
        copy.start()

    def finish(g):
        for n in (0, 1, 3, 2):
            a0_copy(g, n, True).wait_recv()
            put(g, 1 - core, (firsts[g][1] + (n1 - n)) % n1)

    pre_act = None
    for a in range(3):
        term = jnp.dot(slab(st_i, a), b1[a * K3:(a + 1) * K3, :], preferred_element_type=jnp.float32)
        pre_act = term if pre_act is None else pre_act + term
    sigma = 1.0 / (1.0 + jnp.exp(-pre_act))
    hid_t[...] = (pre_act * sigma * keep).T.astype(jnp.bfloat16)
    corr(0, hid_t, lambda a: slab(st_g, 2 - a))
    back = conv_back(st_g, w2r)
    pre_grad = back * sigma * (1.0 + pre_act * (1.0 - sigma)) * keep
    fill_own(pad_p, pre_grad)
    pg_t[...] = pre_grad.T.astype(jnp.bfloat16)
    scatter1(0)
    corr(1, pg_t, lambda a: slab(st_i, a))
    scatter1(1)
    for d in DIRS:
        stage(d, pad_p, send_b, OFFS[INDEX[d]])
    args_b = (send_b, recv_b, hb_sems, 1)
    halo_start(*args_b)
    scatter2(0)
    scatter2(1)
    scatter3(0)
    halo_wait(*args_b)
    for d in DIRS:
        fill_halo(d, pad_p, recv_b, OFFS[INDEX[d]])
    build(pad_p, st_p, True)
    scatter3(1)
    result = conv_back(st_p, w1r)
    fg[...] = ((cot[...].astype(jnp.float32) * keep + result) * keep).astype(jnp.bfloat16)
    fg_copy = pltpu.make_async_copy(fg, fg_out, load_sem.at[0])
    fg_copy.start()
    gather2(0)
    gather2(1)
    gather1(0)
    gather1(1)
    gather0(0)
    gather0(1)
    finish(0)
    finish(1)

    halo_sent(*args_a)
    halo_sent(*args_b)
    for g in range(2):
        sent(r0.at[g], g, "pair")
        sent(s1_send.at[g], g, "s1")
        sent(s2_send.at[g], g, "s2")
        sent(z_all.at[g, pl.ds(0, nz - 1)], g, "zs")
        sent(s1_send.at[g, 0], g, "a2")
        sent(s1_send.at[g], g, "a1")
        sent(ag.at[g, core], g, "a0")
    fg_copy.wait()
    pltpu.make_async_copy(ag, ag_out, out_sem.at[0]).wait()


def unpack_kernel(plan, ag_hbm, fg_hbm, g1_hbm, g2_hbm, fg_out, ag, fg, g1, g2, sems, store_sem):
    n1, r1, t2 = plan.nx, plan.r1, plan.t2
    rows = r1 * TAPS
    blocks = [(half, block) for half in range(2) for block in range(n1)]

    def load(g, half, block):
        return pltpu.make_async_copy(ag_hbm.at[g, half, block], ag.at[g, half, block], sems.at[g, half, block])

    for g in range(2):
        for half, block in blocks:
            load(g, half, block).start()
    load_fg = pltpu.make_async_copy(fg_hbm, fg, store_sem.at[2])
    load_fg.start()
    for half, block in blocks:
        load(0, half, block).wait()
        first = (half * n1 + block) * rows
        for tap in range(TAPS):
            g2[pl.ds(first + tap, r1, stride=TAPS), :] = (
                ag[0, half, block, tap // t2, :, pl.ds(tap % t2 * C, C)].astype(jnp.float32)
            )
        pltpu.make_async_copy(g2.at[pl.ds(first, rows)], g2_hbm.at[pl.ds(first, rows)], store_sem.at[0]).start()
    for half, block in blocks:
        load(1, half, block).wait()
    for tap in range(TAPS):
        square = ag[1, :, :, tap // t2, :, pl.ds(tap % t2 * C, C)].reshape(C, C)
        g1[pl.ds(tap, C, stride=TAPS), :] = square.astype(jnp.float32).T
    for n in range(2 * n1):
        part = pl.ds(n * rows, rows)
        pltpu.make_async_copy(g1.at[part], g1_hbm.at[part], store_sem.at[1]).start()
    load_fg.wait()
    store_fg = pltpu.make_async_copy(fg, fg_out, store_sem.at[2])
    store_fg.start()
    pltpu.make_async_copy(g2, g2_hbm, store_sem.at[0]).wait()
    pltpu.make_async_copy(g1, g1_hbm, store_sem.at[1]).wait()
    store_fg.wait()


def on_device(plan, features, tile_mask, w_first, w_second, cotangent):
    n1, n2, nz, r1, t2 = plan.nx, plan.ny, plan.nz, plan.r1, plan.t2
    f32, bf16 = jnp.float32, jnp.bfloat16
    rows = TAPS * C
    gathered = (2, 2, n1, n2, r1, t2 * C)
    s1_buf = pltpu.VMEM((2, n2, n1 - 1, r1, t2 * C), bf16)
    s2_buf = pltpu.VMEM((2, n2 - 1, r1, t2 * C), f32)
    pad = pltpu.VMEM(((T + 2) * (T + 2) * ZS, C), f32)
    stacked = pltpu.VMEM((T + 2, 64, K3), bf16)
    halo_a = pltpu.VMEM((2 * TILES, 8, C), bf16)
    halo_b = pltpu.VMEM((TILES, 8, C), bf16)
    dma = pltpu.SemaphoreType.DMA
    any_spec = pl.BlockSpec(memory_space=pl.ANY)
    scratch = [
        pltpu.VMEM((512, C), bf16), pltpu.VMEM((512, C), bf16),
        pltpu.VMEM((rows, C), bf16), pltpu.VMEM((rows, C), bf16), pltpu.VMEM((rows, C), f32),
        pltpu.VMEM((C, rows), bf16), pltpu.VMEM((C, rows), bf16), pltpu.VMEM((rows, C), bf16),
        pad, pad, pad, stacked, stacked, stacked,
        halo_a, halo_a, halo_b, halo_b,
        pltpu.VMEM((C, 512), bf16), pltpu.VMEM((C, 512), bf16),
        pltpu.VMEM((2, n2, C, t2 * C), f32), pltpu.VMEM((2, n2, 64, t2 * C), f32),
        s1_buf, s1_buf, pltpu.VMEM((2, r1, t2 * C), f32), s2_buf, s2_buf,
        pltpu.VMEM((2, nz, r1, t2 * C), bf16),
        pltpu.VMEM(gathered, bf16), pltpu.VMEM((512, C), bf16),
        dma((4,)), dma((1,)), dma((2,)), dma((2,)), dma((2, 7)), dma((2, 3 * n2 + 2 * n1)),
    ]
    partial_fg, partial_ag = pl.pallas_call(
        functools.partial(kernel, plan),
        out_shape=(jax.ShapeDtypeStruct((512, C), bf16), jax.ShapeDtypeStruct(gathered, bf16)),
        in_specs=[pl.BlockSpec(memory_space=pltpu.SMEM)] + [any_spec] * 4,
        out_specs=(any_spec,) * 2,
        scratch_shapes=scratch,
        compiler_params=pltpu.CompilerParams(collective_id=0, has_side_effects=True),
        name="block_backward",
    )(tile_mask, features[0], cotangent[0], w_first, w_second)
    grad_first, grad_second, feature_grad = pl.pallas_call(
        functools.partial(unpack_kernel, plan),
        out_shape=(
            jax.ShapeDtypeStruct((rows, C), f32),
            jax.ShapeDtypeStruct((rows, C), f32),
            jax.ShapeDtypeStruct((512, C), bf16),
        ),
        in_specs=[any_spec] * 2,
        out_specs=(any_spec,) * 3,
        scratch_shapes=[
            pltpu.VMEM(gathered, bf16), pltpu.VMEM((512, C), bf16),
            pltpu.VMEM((rows, C), f32), pltpu.VMEM((rows, C), f32), dma((2, 2, n1)), dma((3,)),
        ],
        name="unpack",
    )(partial_ag, partial_fg)
    return grad_first, grad_second, feature_grad[None]


def solution(mesh):
    blocks = mesh.shape["blk"]
    ny = nx = 4 if blocks >= 16 else 2
    plan = Plan(blocks // (nx * ny), nx, ny)
    in_specs = (P("dp", "blk", None), P("dp", "blk"), P(), P(), P("dp", "blk", None))
    out_specs = (P(), P(), P("dp", "blk", None))
    return jax.shard_map(
        functools.partial(on_device, plan), mesh=mesh, in_specs=in_specs, out_specs=out_specs, check_vma=False
    )
```

```python
import functools

import jax
import jax.numpy as jnp
from jax import lax
from jax.experimental import pallas as pl
from jax.experimental.pallas import tpu as pltpu
from jax.sharding import PartitionSpec as P

T = 8
C = 128
TAPS = 27
K3 = 9 * C
UNSCALE = 1.0 / 512.0
ZS = 24
MESH = pl.DeviceIdType.MESH

DIRS = [
    (i, j, k)
    for i in (-1, 0, 1)
    for j in (-1, 0, 1)
    for k in (-1, 0, 1)
    if (i, j, k) != (0, 0, 0)
]
DIRS.sort(key=lambda d: -sum(abs(v) for v in d))
SIZES = [T if sum(abs(v) for v in d) == 1 else 1 for d in DIRS]
OFFS = [sum(SIZES[:n]) for n in range(len(DIRS))]
TILES = sum(SIZES)
INDEX = {d: n for n, d in enumerate(DIRS)}


def opposite(d):
    return (-d[0], -d[1], -d[2])


def boundary_tiles(d, halo):
    def at(v):
        if halo:
            return 0 if v < 0 else T + 1
        return 1 if v < 0 else T

    dx, dy, dz = d
    xs = range(1, T + 1) if dx == 0 else [at(dx)]
    ys = range(1, T + 1) if dy == 0 else [at(dy)]
    row = lambda x, y, z: (x * (T + 2) + y) * ZS + z + 7
    if dz == 0:
        return [(row(x, y, 1), 1, T) for x in xs for y in ys]
    z = at(dz)
    if dy == 0:
        return [(row(x, 1, z), ZS, T) for x in xs]
    if dx == 0:
        return [(row(1, ys[0], z), (T + 2) * ZS, T)]
    return [(row(xs[0], ys[0], z), 1, 1)]


def rows_of(start, stride, size):
    return pl.ds(start, size) if stride == 1 else pl.ds(start, size, stride=stride)


class Plan:
    def __init__(self, nz, nx, ny):
        self.nz, self.nx, self.ny = nz, nx, ny
        self.n1 = nx
        self.r1 = 64 // nx
        self.t2 = -(-TAPS // ny)


def kernel(
    plan,
    mask_ref, feat_hbm, cot_hbm, w1_hbm, w2_hbm,
    fg, ag,
    feat, cot, w1, w2, wf, w1r, w2r, b1,
    pad_i, pad_g, pad_p, st_i, st_g, st_p,
    send_a, recv_a, send_b, recv_b,
    pg_t, hid_t,
    grads, r0, s1_send, s1_recv, s1_own, s2_send, s2_recv, z_all,
    load_sem, ha_sems, hb_sems, red_send, red_recv,
):
    nz, nx, ny = plan.nz, plan.nx, plan.ny
    n1, n2, r1, t2 = nx, ny, plan.r1, plan.t2
    core = lax.axis_index("dp")
    blk = lax.axis_index("blk")
    cz = blk // (nx * ny)
    cx = (blk // ny) % nx
    cy = blk % ny

    loads = [
        pltpu.make_async_copy(src, dst, load_sem.at[n])
        for n, (src, dst) in enumerate(((feat_hbm, feat), (cot_hbm, cot), (w1_hbm, w1), (w2_hbm, w2)))
    ]
    for copy in loads:
        copy.start()

    step1 = ny - (ny - 1) * core
    step2 = 1 + (ny - 1) * core
    c1 = cx + (cy - cx) * core
    c2 = cy + (cx - cy) * core
    base1 = blk - c1 * step1
    base2 = blk - c2 * step2
    plane = blk - cz * (nx * ny)

    def peer1(k):
        return (core, base1 + (c1 + k) % n1 * step1)

    def peer2(k):
        return (core, base2 + (c2 + k) % n2 * step2)

    def peerz(k):
        return (core, plane + (cz + k) % nz * (nx * ny))

    partner = (1 - core, blk)

    def valid(d):
        inside = None
        for place, count, v in ((cz, nz, d[0]), (cx, nx, d[1]), (cy, ny, d[2])):
            if v == 0:
                continue
            test = place < count - 1 if v > 0 else place > 0
            inside = test if inside is None else jnp.logical_and(inside, test)
        return inside

    inside = {d: valid(d).astype(jnp.int32) for d in DIRS}

    def target(d):
        here = inside[d]
        step = d[0] * (nx * ny) + d[1] * ny + d[2]
        return (core + (1 - here) * (1 - 2 * core), blk + here * step)

    barrier = pltpu.get_barrier_semaphore()
    peers = [target(d) for d in DIRS if sum(abs(v) for v in d) > 1]
    peers += [peerz(k) for k in range(1, nz)] + [partner]
    peers += [peer1(k) for k in range(1, n1)] + [peer2(k) for k in range(1, n2)]
    for peer in peers:
        pl.semaphore_signal(barrier, inc=1, device_id=peer, device_id_type=MESH)
    count = len(peers)

    keep = mask_ref[0, 0].astype(jnp.float32)

    def fill_own(pad, values):
        pad3 = pad.reshape((T + 2) * (T + 2), ZS, C)
        for x in range(T):
            pad3[(x + 1) * (T + 2) + 1:(x + 1) * (T + 2) + 1 + T, 8:16, :] = (
                values[x * 64:(x + 1) * 64].reshape(T, T, C)
            )

    def stage(d, pad, send, base):
        for n, (start, stride, size) in enumerate(boundary_tiles(d, False)):
            send[base + n, 0:size] = pad[rows_of(start, stride, size), :].astype(jnp.bfloat16)

    def fill_halo(d, pad, recv, base):
        for n, (start, stride, size) in enumerate(boundary_tiles(d, True)):
            tile = recv[base + n, 0:size].astype(jnp.float32)
            pad[rows_of(start, stride, size), :] = jnp.where(inside[d] > 0, tile, jnp.zeros_like(tile))

    def halo_start(send, recv, sems, arrays):
        for d in DIRS:
            here, there = OFFS[INDEX[d]] * arrays, OFFS[INDEX[opposite(d)]] * arrays
            size = SIZES[INDEX[d]] * arrays
            pltpu.make_async_remote_copy(
                src_ref=send.at[pl.ds(here, size)],
                dst_ref=recv.at[pl.ds(here + inside[d] * (there - here), size)],
                send_sem=sems.at[0], recv_sem=sems.at[1], device_id=target(d), device_id_type=MESH,
            ).start()

    def halo_all(send, recv, sems, arrays):
        return pltpu.make_async_remote_copy(
            src_ref=send, dst_ref=recv, send_sem=sems.at[0], recv_sem=sems.at[1],
            device_id=partner, device_id_type=MESH,
        )

    def halo_wait(*args):
        halo_all(*args).wait_recv()

    def halo_sent(*args):
        halo_all(*args).wait_send()

    def build(pad, stacked, reverse):
        pad3 = pad.reshape((T + 2) * (T + 2), ZS, C)

        def body(x, carry):
            for c in range(3):
                shift_z = 2 - c if reverse else c
                column = pad3[pl.ds(x * (T + 2), T + 2), 7 + shift_z:15 + shift_z, :]
                for b in range(3):
                    shift_y = 2 - b if reverse else b
                    lanes = (3 * b + c) * C
                    stacked[x, :, lanes:lanes + C] = (
                        column[shift_y:shift_y + T].reshape(64, C).astype(jnp.bfloat16)
                    )
            return carry

        lax.fori_loop(0, T + 2, body, 0)

    def slab(stacked, a):
        return stacked[a:a + T].reshape(512, K3)

    loads[0].wait()
    loads[1].wait()
    inputs = feat[...].astype(jnp.float32) * keep
    grads_out = cot[...].astype(jnp.float32) * keep
    fill_own(pad_i, inputs)
    fill_own(pad_g, grads_out)
    for d in DIRS:
        size = SIZES[INDEX[d]]
        stage(d, pad_i, send_a, OFFS[INDEX[d]] * 2)
        stage(d, pad_g, send_a, OFFS[INDEX[d]] * 2 + size)
    pl.semaphore_wait(barrier, count)
    args_a = (send_a, recv_a, ha_sems, 2)
    halo_start(*args_a)

    for g in range(2):
        grads[g, n2 - 1, :, (TAPS - (n2 - 1) * t2) * C:] = jnp.zeros((C, (n2 * t2 - TAPS) * C), jnp.float32)
    loads[2].wait()
    loads[3].wait()
    for w, arranged, stacked in ((w1, w1r, b1), (w2, w2r, None)):
        wf[...] = w[...].astype(jnp.float32)

        def arrange(n, carry):
            row = pl.multiple_of(n * 16, 16)
            for tap in range(TAPS):
                part = wf[pl.ds(n * (16 * TAPS) + tap, 16, stride=TAPS), :].astype(jnp.bfloat16)
                arranged[pl.ds(row, 16), tap * C:(tap + 1) * C] = part
                if stacked is not None:
                    stacked[pl.ds(pl.multiple_of(tap * C + n * 16, 16), 16), :] = part
            return carry

        lax.fori_loop(0, C // 16, arrange, 0)

    halo_wait(*args_a)
    for d in DIRS:
        size = SIZES[INDEX[d]]
        fill_halo(d, pad_i, recv_a, OFFS[INDEX[d]] * 2)
        fill_halo(d, pad_g, recv_a, OFFS[INDEX[d]] * 2 + size)
    build(pad_i, st_i, False)
    build(pad_g, st_g, True)

    def conv_back(stacked, weight):
        total = None
        for a in range(3):
            term = lax.dot_general(
                slab(stacked, 2 - a), weight[:, a * K3:(a + 1) * K3],
                (((1,), (1,)), ((), ())), preferred_element_type=jnp.float32,
            )
            total = term if total is None else total + term
        return total

    recv_first = dict(pair=0, s1=n2, s2=2 * n2, zs=2 * n2 + 1, a2=2 * n2 + 2, a1=3 * n2 + 1, a0=3 * n2 + n1)
    send_index = {name: n for n, name in enumerate(recv_first)}

    def remote(src, dst, g, name, n, peer):
        return pltpu.make_async_remote_copy(
            src_ref=src, dst_ref=dst,
            send_sem=red_send.at[g, send_index[name]], recv_sem=red_recv.at[g, recv_first[name] + n],
            device_id=peer, device_id_type=MESH,
        )

    def arrived(ref, g, name, n=0):
        remote(ref, ref, g, name, n, partner).wait_recv()

    def sent(ref, g, name):
        remote(ref, ref, g, name, 0, partner).wait_send()

    def go(copy):
        copy.start()

    mine = pl.multiple_of(core * 64, 64)
    other = pl.multiple_of(64 - core * 64, 64)
    firsts = ((c2, c1), (c1, c2))
    hop1 = (peer2, peer1)
    hop2 = (peer1, peer2)

    def chunk(g, i):
        own = firsts[g][1]
        return own if i == n2 - 1 else i + (i >= own).astype(jnp.int32)

    def pair_copy(g, j):
        return remote(grads.at[g, j, pl.ds(other, 64)], r0.at[g, j], g, "pair", j, partner)

    def chip(g, j, block):
        here = pl.multiple_of(block % n1 * r1, r1)
        return grads[g, j, pl.ds(mine + here, r1), :] + r0[g, j, pl.ds(here, r1), :]

    def s1_copy(g, i, k):
        return remote(s1_send.at[g, i, k - 1], s1_recv.at[g, i, k - 1], g, "s1", i, hop1[g](k))

    def s2_copy(g, i):
        k = (chunk(g, i) - firsts[g][1] + n2) % n2
        return remote(s2_send.at[g, i], s2_recv.at[g, k - 1], g, "s2", 0, hop2[g](k))

    def z_copy(g, k):
        ref = z_all.at[g, cz]
        return remote(ref, ref, g, "zs", 0, peerz(k))

    def a2_copy(g, k, wait):
        b, j = firsts[g]
        ref = ag.at[g, core, b, (j + (n2 - k)) % n2 if wait else j]
        return remote(ref, ref, g, "a2", k - 1, hop2[g](k))

    def a1_copy(g, m, k):
        b, j = firsts[g]
        ref = ag.at[g, core, b, (j + (n2 - m)) % n2]
        return remote(ref, ref, g, "a1", k - 1, hop1[g](k))

    def a0_copy(g, n, wait):
        ref = ag.at[g, 1 - core if wait else core, (firsts[g][1 if wait else 0] + (n1 - n)) % n1]
        return remote(ref, ref, g, "a0", n, partner)

    def corr(g, lhs_t, slab_of):
        sent = 0
        for a in range(3):
            part = jnp.dot(lhs_t[...], slab_of(a), preferred_element_type=jnp.float32)
            for n in range(9):
                tap = 9 * a + n
                at = tap % t2 * C
                grads[g, tap // t2, :, at:at + C] = part[:, n * C:(n + 1) * C]
            while sent < n2 and min((sent + 1) * t2, TAPS) <= 9 * (a + 1):
                go(pair_copy(g, sent))
                sent += 1

    far_first = (2, 1, 3)

    def scatter1(g):
        for i in range(n2):
            j = chunk(g, i)
            pair_copy(g, j).wait_recv()
            for k in far_first:
                s1_send[g, i, k - 1] = chip(g, j, firsts[g][0] + k).astype(jnp.bfloat16)
                go(s1_copy(g, i, k))

    def scatter2(g):
        for i in range(n2):
            total = chip(g, chunk(g, i), firsts[g][0])
            arrived(s1_recv.at[g, i], g, "s1", i)
            for k in range(1, n1):
                total = total + s1_recv[g, i, k - 1].astype(jnp.float32)
            if i < n2 - 1:
                s2_send[g, i] = total
                go(s2_copy(g, i))
            else:
                s1_own[g] = total

    z_order = (4, 3, 5, 2, 6, 1, 7)

    def scatter3(g):
        total = s1_own[g]
        arrived(s2_recv.at[g], g, "s2")
        for k in range(1, n2):
            total = total + s2_recv[g, k - 1]
        z_all[g, cz] = total.astype(jnp.bfloat16)
        for k in z_order:
            go(z_copy(g, k))

    def gather2(g):
        arrived(z_all.at[g, pl.ds(0, nz - 1)], g, "zs")
        total = z_all[g, 0].astype(jnp.float32)
        for z in range(1, nz):
            total = total + z_all[g, z].astype(jnp.float32)
        b, j = firsts[g]
        ag[g, core, b, j] = (total * UNSCALE).astype(jnp.bfloat16)
        for k in far_first:
            go(a2_copy(g, k, False))
        for k in far_first:
            go(a1_copy(g, 0, k))

    def gather1(g):
        for m in (1, 3, 2):
            a2_copy(g, m, True).wait_recv()
            for k in far_first:
                go(a1_copy(g, m, k))
        go(a0_copy(g, 0, False))

    def gather0(g):
        for k in (1, 3, 2):
            block = (firsts[g][0] + (n1 - k)) % n1
            arrived(ag.at[g, core, block], g, "a1", k - 1)
            go(a0_copy(g, k, False))

    def finish(g):
        for n in (0, 1, 3, 2):
            a0_copy(g, n, True).wait_recv()

    pre_act = None
    for a in range(3):
        term = jnp.dot(slab(st_i, a), b1[a * K3:(a + 1) * K3, :], preferred_element_type=jnp.float32)
        pre_act = term if pre_act is None else pre_act + term
    sigma = 1.0 / (1.0 + jnp.exp(-pre_act))
    hid_t[...] = (pre_act * sigma * keep).T.astype(jnp.bfloat16)
    corr(0, hid_t, lambda a: slab(st_g, 2 - a))
    back = conv_back(st_g, w2r)
    pre_grad = back * sigma * (1.0 + pre_act * (1.0 - sigma)) * keep
    fill_own(pad_p, pre_grad)
    pg_t[...] = pre_grad.T.astype(jnp.bfloat16)
    scatter1(0)
    corr(1, pg_t, lambda a: slab(st_i, a))
    for d in DIRS:
        stage(d, pad_p, send_b, OFFS[INDEX[d]])
    scatter1(1)
    args_b = (send_b, recv_b, hb_sems, 1)
    halo_start(*args_b)
    scatter2(0)
    scatter2(1)
    scatter3(0)
    halo_wait(*args_b)
    for d in DIRS:
        fill_halo(d, pad_p, recv_b, OFFS[INDEX[d]])
    build(pad_p, st_p, True)
    scatter3(1)
    result = conv_back(st_p, w1r)
    fg[...] = ((cot[...].astype(jnp.float32) * keep + result) * keep).astype(jnp.bfloat16)
    gather2(0)
    gather2(1)
    gather1(0)
    gather1(1)
    gather0(0)
    gather0(1)
    finish(0)
    finish(1)

    halo_sent(*args_a)
    halo_sent(*args_b)
    for g in range(2):
        sent(r0.at[g], g, "pair")
        sent(s1_send.at[g], g, "s1")
        sent(s2_send.at[g], g, "s2")
        sent(z_all.at[g, pl.ds(0, nz - 1)], g, "zs")
        sent(s1_send.at[g, 0], g, "a2")
        sent(s1_send.at[g], g, "a1")
        sent(ag.at[g, core], g, "a0")


def unpack_kernel(plan, ag, fg, g1_hbm, g2_hbm, fg_out, g1, g2, store_sem):
    n1, r1, t2 = plan.nx, plan.r1, plan.t2
    rows = r1 * TAPS
    blocks = [(half, block) for half in range(2) for block in range(n1)]

    store_fg = pltpu.make_async_copy(fg, fg_out, store_sem.at[2])
    store_fg.start()
    for half, block in blocks:
        first = (half * n1 + block) * rows
        for tap in range(TAPS):
            g2[pl.ds(first + tap, r1, stride=TAPS), :] = (
                ag[0, half, block, tap // t2, :, pl.ds(tap % t2 * C, C)].astype(jnp.float32)
            )
        pltpu.make_async_copy(g2.at[pl.ds(first, rows)], g2_hbm.at[pl.ds(first, rows)], store_sem.at[0]).start()
    for tap in range(TAPS):
        square = ag[1, :, :, tap // t2, :, pl.ds(tap % t2 * C, C)].reshape(C, C)
        g1[pl.ds(tap, C, stride=TAPS), :] = square.astype(jnp.float32).T
    for n in range(2 * n1):
        part = pl.ds(n * rows, rows)
        pltpu.make_async_copy(g1.at[part], g1_hbm.at[part], store_sem.at[1]).start()
    pltpu.make_async_copy(g2, g2_hbm, store_sem.at[0]).wait()
    pltpu.make_async_copy(g1, g1_hbm, store_sem.at[1]).wait()
    store_fg.wait()


def on_device(plan, features, tile_mask, w_first, w_second, cotangent):
    n1, n2, nz, r1, t2 = plan.nx, plan.ny, plan.nz, plan.r1, plan.t2
    f32, bf16 = jnp.float32, jnp.bfloat16
    rows = TAPS * C
    gathered = (2, 2, n1, n2, r1, t2 * C)
    s1_buf = pltpu.VMEM((2, n2, n1 - 1, r1, t2 * C), bf16)
    s2_buf = pltpu.VMEM((2, n2 - 1, r1, t2 * C), f32)
    pad = pltpu.VMEM(((T + 2) * (T + 2) * ZS, C), f32)
    stacked = pltpu.VMEM((T + 2, 64, K3), bf16)
    halo_a = pltpu.VMEM((2 * TILES, 8, C), bf16)
    halo_b = pltpu.VMEM((TILES, 8, C), bf16)
    dma = pltpu.SemaphoreType.DMA
    vmem_spec = pl.BlockSpec(memory_space=pltpu.VMEM)
    any_spec = pl.BlockSpec(memory_space=pl.ANY)
    scratch = [
        pltpu.VMEM((512, C), bf16), pltpu.VMEM((512, C), bf16),
        pltpu.VMEM((rows, C), bf16), pltpu.VMEM((rows, C), bf16), pltpu.VMEM((rows, C), f32),
        pltpu.VMEM((C, rows), bf16), pltpu.VMEM((C, rows), bf16), pltpu.VMEM((rows, C), bf16),
        pad, pad, pad, stacked, stacked, stacked,
        halo_a, halo_a, halo_b, halo_b,
        pltpu.VMEM((C, 512), bf16), pltpu.VMEM((C, 512), bf16),
        pltpu.VMEM((2, n2, C, t2 * C), f32), pltpu.VMEM((2, n2, 64, t2 * C), f32),
        s1_buf, s1_buf, pltpu.VMEM((2, r1, t2 * C), f32), s2_buf, s2_buf,
        pltpu.VMEM((2, nz, r1, t2 * C), bf16),
        dma((4,)), dma((2,)), dma((2,)), dma((2, 7)), dma((2, 3 * n2 + 2 * n1)),
    ]
    partial_fg, partial_ag = pl.pallas_call(
        functools.partial(kernel, plan),
        out_shape=(pltpu.VMEM((512, C), bf16), pltpu.VMEM(gathered, bf16)),
        in_specs=[pl.BlockSpec(memory_space=pltpu.SMEM)] + [any_spec] * 4,
        out_specs=(vmem_spec,) * 2,
        scratch_shapes=scratch,
        compiler_params=pltpu.CompilerParams(
            collective_id=0, has_side_effects=True, vmem_limit_bytes=56 * 1024 * 1024
        ),
        name="block_backward",
    )(tile_mask, features[0], cotangent[0], w_first, w_second)
    grad_first, grad_second, feature_grad = pl.pallas_call(
        functools.partial(unpack_kernel, plan),
        out_shape=(
            jax.ShapeDtypeStruct((rows, C), f32),
            jax.ShapeDtypeStruct((rows, C), f32),
            jax.ShapeDtypeStruct((512, C), bf16),
        ),
        in_specs=[vmem_spec] * 2,
        out_specs=(any_spec,) * 3,
        scratch_shapes=[
            pltpu.VMEM((rows, C), f32), pltpu.VMEM((rows, C), f32), dma((3,)),
        ],
        compiler_params=pltpu.CompilerParams(vmem_limit_bytes=16 * 1024 * 1024),
        name="unpack",
    )(partial_ag, partial_fg)
    return grad_first, grad_second, feature_grad[None]


def solution(mesh):
    blocks = mesh.shape["blk"]
    ny = nx = 4 if blocks >= 16 else 2
    plan = Plan(blocks // (nx * ny), nx, ny)
    in_specs = (P("dp", "blk", None), P("dp", "blk"), P(), P(), P("dp", "blk", None))
    out_specs = (P(), P(), P("dp", "blk", None))
    return jax.shard_map(
        functools.partial(on_device, plan), mesh=mesh, in_specs=in_specs, out_specs=out_specs, check_vma=False
    )
```

```python
import functools

import jax
import jax.numpy as jnp
from jax import lax
from jax.experimental import pallas as pl
from jax.experimental.pallas import tpu as pltpu
from jax.sharding import PartitionSpec as P

T = 8
C = 128
TAPS = 27
K3 = 9 * C
UNSCALE = 1.0 / 512.0
ZS = 24
MESH = pl.DeviceIdType.MESH

DIRS = [
    (i, j, k)
    for i in (-1, 0, 1)
    for j in (-1, 0, 1)
    for k in (-1, 0, 1)
    if (i, j, k) != (0, 0, 0)
]
DIRS.sort(key=lambda d: -sum(abs(v) for v in d))
SIZES = [T if sum(abs(v) for v in d) == 1 else 1 for d in DIRS]
OFFS = [sum(SIZES[:n]) for n in range(len(DIRS))]
TILES = sum(SIZES)
INDEX = {d: n for n, d in enumerate(DIRS)}


def opposite(d):
    return (-d[0], -d[1], -d[2])


def boundary_tiles(d, halo):
    def at(v):
        if halo:
            return 0 if v < 0 else T + 1
        return 1 if v < 0 else T

    dx, dy, dz = d
    xs = range(1, T + 1) if dx == 0 else [at(dx)]
    ys = range(1, T + 1) if dy == 0 else [at(dy)]
    row = lambda x, y, z: (x * (T + 2) + y) * ZS + z + 7
    if dz == 0:
        return [(row(x, y, 1), 1, T) for x in xs for y in ys]
    z = at(dz)
    if dy == 0:
        return [(row(x, 1, z), ZS, T) for x in xs]
    if dx == 0:
        return [(row(1, ys[0], z), (T + 2) * ZS, T)]
    return [(row(xs[0], ys[0], z), 1, 1)]


def rows_of(start, stride, size):
    return pl.ds(start, size) if stride == 1 else pl.ds(start, size, stride=stride)


class Plan:
    def __init__(self, nz, nx, ny):
        self.nz, self.nx, self.ny = nz, nx, ny
        self.n1 = nx
        self.r1 = 64 // nx
        self.t2 = -(-TAPS // ny)


def kernel(
    plan,
    mask_ref, feat_hbm, cot_hbm, w1_hbm, w2_hbm,
    fg, ag,
    feat, cot, w1, w2, wf, w1r, w2r, b1,
    pad_i, pad_g, pad_p, st_i, st_g, st_p,
    send_a, recv_a, send_b, recv_b,
    pg_t, hid_t,
    grads, r0, s1_send, s1_recv, s1_own, s2_send, s2_recv, z_all,
    load_sem, ha_sems, hb_sems, red_send, red_recv,
):
    nz, nx, ny = plan.nz, plan.nx, plan.ny
    n1, n2, r1, t2 = nx, ny, plan.r1, plan.t2
    core = lax.axis_index("dp")
    blk = lax.axis_index("blk")
    cz = blk // (nx * ny)
    cx = (blk // ny) % nx
    cy = blk % ny

    loads = [
        pltpu.make_async_copy(src, dst, load_sem.at[n])
        for n, (src, dst) in enumerate(((feat_hbm, feat), (cot_hbm, cot), (w1_hbm, w1), (w2_hbm, w2)))
    ]
    for copy in loads:
        copy.start()

    step1 = ny - (ny - 1) * core
    step2 = 1 + (ny - 1) * core
    c1 = cx + (cy - cx) * core
    c2 = cy + (cx - cy) * core
    base1 = blk - c1 * step1
    base2 = blk - c2 * step2
    plane = blk - cz * (nx * ny)

    def peer1(k):
        return (core, base1 + (c1 + k) % n1 * step1)

    def peer2(k):
        return (core, base2 + (c2 + k) % n2 * step2)

    def peerz(k):
        return (core, plane + (cz + k) % nz * (nx * ny))

    partner = (1 - core, blk)

    def valid(d):
        inside = None
        for place, count, v in ((cz, nz, d[0]), (cx, nx, d[1]), (cy, ny, d[2])):
            if v == 0:
                continue
            test = place < count - 1 if v > 0 else place > 0
            inside = test if inside is None else jnp.logical_and(inside, test)
        return inside

    inside = {d: valid(d).astype(jnp.int32) for d in DIRS}

    def target(d):
        here = inside[d]
        step = d[0] * (nx * ny) + d[1] * ny + d[2]
        return (core + (1 - here) * (1 - 2 * core), blk + here * step)

    barrier = pltpu.get_barrier_semaphore()
    peers = [target(d) for d in DIRS if sum(abs(v) for v in d) > 1]
    peers += [peerz(k) for k in range(1, nz)] + [partner]
    peers += [peer1(k) for k in range(1, n1)] + [peer2(k) for k in range(1, n2)]
    for peer in peers:
        pl.semaphore_signal(barrier, inc=1, device_id=peer, device_id_type=MESH)
    count = len(peers)

    keep = mask_ref[0, 0].astype(jnp.float32)

    def fill_own(pad, values):
        pad3 = pad.reshape((T + 2) * (T + 2), ZS, C)
        for x in range(T):
            pad3[(x + 1) * (T + 2) + 1:(x + 1) * (T + 2) + 1 + T, 8:16, :] = (
                values[x * 64:(x + 1) * 64].reshape(T, T, C)
            )

    def stage(d, pad, send, base):
        for n, (start, stride, size) in enumerate(boundary_tiles(d, False)):
            send[base + n, 0:size] = pad[rows_of(start, stride, size), :].astype(jnp.bfloat16)

    def fill_halo(d, pad, recv, base):
        for n, (start, stride, size) in enumerate(boundary_tiles(d, True)):
            tile = recv[base + n, 0:size].astype(jnp.float32)
            pad[rows_of(start, stride, size), :] = jnp.where(inside[d] > 0, tile, jnp.zeros_like(tile))

    def halo_start(send, recv, sems, arrays):
        for d in DIRS:
            here, there = OFFS[INDEX[d]] * arrays, OFFS[INDEX[opposite(d)]] * arrays
            size = SIZES[INDEX[d]] * arrays
            pltpu.make_async_remote_copy(
                src_ref=send.at[pl.ds(here, size)],
                dst_ref=recv.at[pl.ds(here + inside[d] * (there - here), size)],
                send_sem=sems.at[0], recv_sem=sems.at[1], device_id=target(d), device_id_type=MESH,
            ).start()

    def halo_all(send, recv, sems, arrays):
        return pltpu.make_async_remote_copy(
            src_ref=send, dst_ref=recv, send_sem=sems.at[0], recv_sem=sems.at[1],
            device_id=partner, device_id_type=MESH,
        )

    def halo_wait(*args):
        halo_all(*args).wait_recv()

    def halo_sent(*args):
        halo_all(*args).wait_send()

    def build(pad, stacked, reverse):
        pad3 = pad.reshape((T + 2) * (T + 2), ZS, C)

        def body(x, carry):
            for c in range(3):
                shift_z = 2 - c if reverse else c
                column = pad3[pl.ds(x * (T + 2), T + 2), 7 + shift_z:15 + shift_z, :]
                for b in range(3):
                    shift_y = 2 - b if reverse else b
                    lanes = (3 * b + c) * C
                    stacked[x, :, lanes:lanes + C] = (
                        column[shift_y:shift_y + T].reshape(64, C).astype(jnp.bfloat16)
                    )
            return carry

        lax.fori_loop(0, T + 2, body, 0)

    def slab(stacked, a):
        return stacked[a:a + T].reshape(512, K3)

    loads[0].wait()
    loads[1].wait()
    inputs = feat[...].astype(jnp.float32) * keep
    grads_out = cot[...].astype(jnp.float32) * keep
    fill_own(pad_i, inputs)
    fill_own(pad_g, grads_out)
    for d in DIRS:
        size = SIZES[INDEX[d]]
        stage(d, pad_i, send_a, OFFS[INDEX[d]] * 2)
        stage(d, pad_g, send_a, OFFS[INDEX[d]] * 2 + size)
    pl.semaphore_wait(barrier, count)
    args_a = (send_a, recv_a, ha_sems, 2)
    halo_start(*args_a)

    for g in range(2):
        grads[g, n2 - 1, :, (TAPS - (n2 - 1) * t2) * C:] = jnp.zeros((C, (n2 * t2 - TAPS) * C), jnp.float32)
    loads[2].wait()
    loads[3].wait()
    for w, arranged, stacked in ((w1, w1r, b1), (w2, w2r, None)):
        wf[...] = w[...].astype(jnp.float32)

        def arrange(n, carry):
            row = pl.multiple_of(n * 16, 16)
            for tap in range(TAPS):
                part = wf[pl.ds(n * (16 * TAPS) + tap, 16, stride=TAPS), :].astype(jnp.bfloat16)
                arranged[pl.ds(row, 16), tap * C:(tap + 1) * C] = part
                if stacked is not None:
                    stacked[pl.ds(pl.multiple_of(tap * C + n * 16, 16), 16), :] = part
            return carry

        lax.fori_loop(0, C // 16, arrange, 0)

    halo_wait(*args_a)
    for d in DIRS:
        size = SIZES[INDEX[d]]
        fill_halo(d, pad_i, recv_a, OFFS[INDEX[d]] * 2)
        fill_halo(d, pad_g, recv_a, OFFS[INDEX[d]] * 2 + size)
    build(pad_i, st_i, False)
    build(pad_g, st_g, True)

    def conv_back(stacked, weight):
        total = None
        for a in range(3):
            term = lax.dot_general(
                slab(stacked, 2 - a), weight[:, a * K3:(a + 1) * K3],
                (((1,), (1,)), ((), ())), preferred_element_type=jnp.float32,
            )
            total = term if total is None else total + term
        return total

    recv_first = dict(pair=0, s1=n2, s2=2 * n2, zs=2 * n2 + 1, a2=2 * n2 + 2, a1=3 * n2 + 1, a0=3 * n2 + n1)
    send_index = {name: n for n, name in enumerate(recv_first)}

    def remote(src, dst, g, name, n, peer):
        return pltpu.make_async_remote_copy(
            src_ref=src, dst_ref=dst,
            send_sem=red_send.at[g, send_index[name]], recv_sem=red_recv.at[g, recv_first[name] + n],
            device_id=peer, device_id_type=MESH,
        )

    def arrived(ref, g, name, n=0):
        remote(ref, ref, g, name, n, partner).wait_recv()

    def sent(ref, g, name):
        remote(ref, ref, g, name, 0, partner).wait_send()

    def go(copy):
        copy.start()

    mine = pl.multiple_of(core * 64, 64)
    other = pl.multiple_of(64 - core * 64, 64)
    firsts = ((c2, c1), (c1, c2))
    hop1 = (peer2, peer1)
    hop2 = (peer1, peer2)

    def chunk(g, i):
        own = firsts[g][1]
        return own if i == n2 - 1 else i + (i >= own).astype(jnp.int32)

    def pair_copy(g, j):
        return remote(grads.at[g, j, pl.ds(other, 64)], r0.at[g, j], g, "pair", j, partner)

    def chip(g, j, block):
        here = pl.multiple_of(block % n1 * r1, r1)
        return grads[g, j, pl.ds(mine + here, r1), :] + r0[g, j, pl.ds(here, r1), :]

    def s1_copy(g, i, k):
        return remote(s1_send.at[g, i, k - 1], s1_recv.at[g, i, k - 1], g, "s1", i, hop1[g](k))

    def s2_copy(g, i):
        k = (chunk(g, i) - firsts[g][1] + n2) % n2
        return remote(s2_send.at[g, i], s2_recv.at[g, k - 1], g, "s2", 0, hop2[g](k))

    def z_copy(g, k):
        ref = z_all.at[g, cz]
        return remote(ref, ref, g, "zs", 0, peerz(k))

    def a2_copy(g, k, wait):
        b, j = firsts[g]
        ref = ag.at[g, core, b, (j + (n2 - k)) % n2 if wait else j]
        return remote(ref, ref, g, "a2", k - 1, hop2[g](k))

    def a1_copy(g, m, k):
        b, j = firsts[g]
        ref = ag.at[g, core, b, (j + (n2 - m)) % n2]
        return remote(ref, ref, g, "a1", k - 1, hop1[g](k))

    def a0_copy(g, n, wait):
        ref = ag.at[g, 1 - core if wait else core, (firsts[g][1 if wait else 0] + (n1 - n)) % n1]
        return remote(ref, ref, g, "a0", n, partner)

    def corr(g, lhs_t, slab_of):
        sent = 0
        for a in range(3):
            part = jnp.dot(lhs_t[...], slab_of(a), preferred_element_type=jnp.float32)
            for n in range(9):
                tap = 9 * a + n
                at = tap % t2 * C
                grads[g, tap // t2, :, at:at + C] = part[:, n * C:(n + 1) * C]
            while sent < n2 and min((sent + 1) * t2, TAPS) <= 9 * (a + 1):
                go(pair_copy(g, sent))
                sent += 1

    far_first = (3, 2, 1)

    def scatter1(g):
        for i in range(n2):
            j = chunk(g, i)
            pair_copy(g, j).wait_recv()
            for k in far_first:
                s1_send[g, i, k - 1] = chip(g, j, firsts[g][0] + k).astype(jnp.bfloat16)
                go(s1_copy(g, i, k))

    def scatter2(g):
        for i in range(n2):
            total = chip(g, chunk(g, i), firsts[g][0])
            arrived(s1_recv.at[g, i], g, "s1", i)
            for k in range(1, n1):
                total = total + s1_recv[g, i, k - 1].astype(jnp.float32)
            if i < n2 - 1:
                s2_send[g, i] = total.astype(jnp.bfloat16)
                go(s2_copy(g, i))
            else:
                s1_own[g] = total

    z_order = (4, 3, 5, 2, 6, 1, 7)

    def scatter3(g):
        total = s1_own[g]
        arrived(s2_recv.at[g], g, "s2")
        for k in range(1, n2):
            total = total + s2_recv[g, k - 1].astype(jnp.float32)
        z_all[g, cz] = total.astype(jnp.bfloat16)
        for k in z_order:
            go(z_copy(g, k))

    def gather2(g):
        arrived(z_all.at[g, pl.ds(0, nz - 1)], g, "zs")
        total = z_all[g, 0].astype(jnp.float32)
        for z in range(1, nz):
            total = total + z_all[g, z].astype(jnp.float32)
        b, j = firsts[g]
        ag[g, core, b, j] = (total * UNSCALE).astype(jnp.bfloat16)
        for k in far_first:
            go(a2_copy(g, k, False))
        for k in far_first:
            go(a1_copy(g, 0, k))

    def gather1(g):
        for m in (1, 3, 2):
            a2_copy(g, m, True).wait_recv()
            for k in far_first:
                go(a1_copy(g, m, k))
        go(a0_copy(g, 0, False))

    def gather0(g):
        for k in (1, 3, 2):
            block = (firsts[g][0] + (n1 - k)) % n1
            arrived(ag.at[g, core, block], g, "a1", k - 1)
            go(a0_copy(g, k, False))

    def finish(g):
        for n in (0, 1, 3, 2):
            a0_copy(g, n, True).wait_recv()

    pre_act = None
    for a in range(3):
        term = jnp.dot(slab(st_i, a), b1[a * K3:(a + 1) * K3, :], preferred_element_type=jnp.float32)
        pre_act = term if pre_act is None else pre_act + term
    sigma = 1.0 / (1.0 + jnp.exp(-pre_act))
    hid_t[...] = (pre_act * sigma * keep).T.astype(jnp.bfloat16)
    corr(0, hid_t, lambda a: slab(st_g, 2 - a))
    back = conv_back(st_g, w2r)
    pre_grad = back * sigma * (1.0 + pre_act * (1.0 - sigma)) * keep
    fill_own(pad_p, pre_grad)
    pg_t[...] = pre_grad.T.astype(jnp.bfloat16)
    scatter1(0)
    corr(1, pg_t, lambda a: slab(st_i, a))
    for d in DIRS:
        stage(d, pad_p, send_b, OFFS[INDEX[d]])
    scatter1(1)
    args_b = (send_b, recv_b, hb_sems, 1)
    halo_start(*args_b)
    scatter2(0)
    scatter2(1)
    scatter3(0)
    halo_wait(*args_b)
    for d in DIRS:
        fill_halo(d, pad_p, recv_b, OFFS[INDEX[d]])
    build(pad_p, st_p, True)
    scatter3(1)
    result = conv_back(st_p, w1r)
    fg[...] = ((cot[...].astype(jnp.float32) * keep + result) * keep).astype(jnp.bfloat16)
    gather2(0)
    gather2(1)
    gather1(0)
    gather1(1)
    gather0(0)
    gather0(1)
    finish(0)
    finish(1)

    halo_sent(*args_a)
    halo_sent(*args_b)
    for g in range(2):
        sent(r0.at[g], g, "pair")
        sent(s1_send.at[g], g, "s1")
        sent(s2_send.at[g], g, "s2")
        sent(z_all.at[g, pl.ds(0, nz - 1)], g, "zs")
        sent(s1_send.at[g, 0], g, "a2")
        sent(s1_send.at[g], g, "a1")
        sent(ag.at[g, core], g, "a0")


def unpack_kernel(plan, ag, fg, g1_hbm, g2_hbm, fg_out, g1, g2, store_sem):
    n1, r1, t2 = plan.nx, plan.r1, plan.t2
    rows = r1 * TAPS
    blocks = [(half, block) for half in range(2) for block in range(n1)]

    store_fg = pltpu.make_async_copy(fg, fg_out, store_sem.at[2])
    store_fg.start()
    for half, block in blocks:
        first = (half * n1 + block) * rows
        for tap in range(TAPS):
            g2[pl.ds(first + tap, r1, stride=TAPS), :] = (
                ag[0, half, block, tap // t2, :, pl.ds(tap % t2 * C, C)].astype(jnp.float32)
            )
        pltpu.make_async_copy(g2.at[pl.ds(first, rows)], g2_hbm.at[pl.ds(first, rows)], store_sem.at[0]).start()
    for tap in range(TAPS):
        square = ag[1, :, :, tap // t2, :, pl.ds(tap % t2 * C, C)].reshape(C, C)
        g1[pl.ds(tap, C, stride=TAPS), :] = square.astype(jnp.float32).T
    for n in range(2 * n1):
        part = pl.ds(n * rows, rows)
        pltpu.make_async_copy(g1.at[part], g1_hbm.at[part], store_sem.at[1]).start()
    pltpu.make_async_copy(g2, g2_hbm, store_sem.at[0]).wait()
    pltpu.make_async_copy(g1, g1_hbm, store_sem.at[1]).wait()
    store_fg.wait()


def on_device(plan, features, tile_mask, w_first, w_second, cotangent):
    n1, n2, nz, r1, t2 = plan.nx, plan.ny, plan.nz, plan.r1, plan.t2
    f32, bf16 = jnp.float32, jnp.bfloat16
    rows = TAPS * C
    gathered = (2, 2, n1, n2, r1, t2 * C)
    s1_buf = pltpu.VMEM((2, n2, n1 - 1, r1, t2 * C), bf16)
    s2_buf = pltpu.VMEM((2, n2 - 1, r1, t2 * C), bf16)
    pad = pltpu.VMEM(((T + 2) * (T + 2) * ZS, C), f32)
    stacked = pltpu.VMEM((T + 2, 64, K3), bf16)
    halo_a = pltpu.VMEM((2 * TILES, 8, C), bf16)
    halo_b = pltpu.VMEM((TILES, 8, C), bf16)
    dma = pltpu.SemaphoreType.DMA
    vmem_spec = pl.BlockSpec(memory_space=pltpu.VMEM)
    any_spec = pl.BlockSpec(memory_space=pl.ANY)
    scratch = [
        pltpu.VMEM((512, C), bf16), pltpu.VMEM((512, C), bf16),
        pltpu.VMEM((rows, C), bf16), pltpu.VMEM((rows, C), bf16), pltpu.VMEM((rows, C), f32),
        pltpu.VMEM((C, rows), bf16), pltpu.VMEM((C, rows), bf16), pltpu.VMEM((rows, C), bf16),
        pad, pad, pad, stacked, stacked, stacked,
        halo_a, halo_a, halo_b, halo_b,
        pltpu.VMEM((C, 512), bf16), pltpu.VMEM((C, 512), bf16),
        pltpu.VMEM((2, n2, C, t2 * C), f32), pltpu.VMEM((2, n2, 64, t2 * C), f32),
        s1_buf, s1_buf, pltpu.VMEM((2, r1, t2 * C), f32), s2_buf, s2_buf,
        pltpu.VMEM((2, nz, r1, t2 * C), bf16),
        dma((4,)), dma((2,)), dma((2,)), dma((2, 7)), dma((2, 3 * n2 + 2 * n1)),
    ]
    partial_fg, partial_ag = pl.pallas_call(
        functools.partial(kernel, plan),
        out_shape=(pltpu.VMEM((512, C), bf16), pltpu.VMEM(gathered, bf16)),
        in_specs=[pl.BlockSpec(memory_space=pltpu.SMEM)] + [any_spec] * 4,
        out_specs=(vmem_spec,) * 2,
        scratch_shapes=scratch,
        compiler_params=pltpu.CompilerParams(
            collective_id=0, has_side_effects=True, vmem_limit_bytes=56 * 1024 * 1024
        ),
        name="block_backward",
    )(tile_mask, features[0], cotangent[0], w_first, w_second)
    grad_first, grad_second, feature_grad = pl.pallas_call(
        functools.partial(unpack_kernel, plan),
        out_shape=(
            jax.ShapeDtypeStruct((rows, C), f32),
            jax.ShapeDtypeStruct((rows, C), f32),
            jax.ShapeDtypeStruct((512, C), bf16),
        ),
        in_specs=[vmem_spec] * 2,
        out_specs=(any_spec,) * 3,
        scratch_shapes=[
            pltpu.VMEM((rows, C), f32), pltpu.VMEM((rows, C), f32), dma((3,)),
        ],
        compiler_params=pltpu.CompilerParams(vmem_limit_bytes=16 * 1024 * 1024),
        name="unpack",
    )(partial_ag, partial_fg)
    return grad_first, grad_second, feature_grad[None]


def solution(mesh):
    blocks = mesh.shape["blk"]
    ny = nx = 4 if blocks >= 16 else 2
    plan = Plan(blocks // (nx * ny), nx, ny)
    in_specs = (P("dp", "blk", None), P("dp", "blk"), P(), P(), P("dp", "blk", None))
    out_specs = (P(), P(), P("dp", "blk", None))
    return jax.shard_map(
        functools.partial(on_device, plan), mesh=mesh, in_specs=in_specs, out_specs=out_specs, check_vma=False
    )
```

```python
import functools

import jax
import jax.numpy as jnp
from jax import lax
from jax.experimental import pallas as pl
from jax.experimental.pallas import tpu as pltpu
from jax.sharding import PartitionSpec as P

T = 8
C = 128
TAPS = 27
K3 = 9 * C
UNSCALE = 1.0 / 512.0
ZS = 24
MESH = pl.DeviceIdType.MESH

DIRS = [
    (i, j, k)
    for i in (-1, 0, 1)
    for j in (-1, 0, 1)
    for k in (-1, 0, 1)
    if (i, j, k) != (0, 0, 0)
]
DIRS.sort(key=lambda d: -sum(abs(v) for v in d))
SIZES = [T if sum(abs(v) for v in d) == 1 else 1 for d in DIRS]
OFFS = [sum(SIZES[:n]) for n in range(len(DIRS))]
TILES = sum(SIZES)
INDEX = {d: n for n, d in enumerate(DIRS)}


def opposite(d):
    return (-d[0], -d[1], -d[2])


def boundary_tiles(d, halo):
    def at(v):
        if halo:
            return 0 if v < 0 else T + 1
        return 1 if v < 0 else T

    dx, dy, dz = d
    xs = range(1, T + 1) if dx == 0 else [at(dx)]
    ys = range(1, T + 1) if dy == 0 else [at(dy)]
    row = lambda x, y, z: (x * (T + 2) + y) * ZS + z + 7
    if dz == 0:
        return [(row(x, y, 1), 1, T) for x in xs for y in ys]
    z = at(dz)
    if dy == 0:
        return [(row(x, 1, z), ZS, T) for x in xs]
    if dx == 0:
        return [(row(1, ys[0], z), (T + 2) * ZS, T)]
    return [(row(xs[0], ys[0], z), 1, 1)]


def rows_of(start, stride, size):
    return pl.ds(start, size) if stride == 1 else pl.ds(start, size, stride=stride)


class Plan:
    def __init__(self, nz, nx, ny):
        self.nz, self.nx, self.ny = nz, nx, ny
        self.n1 = nx
        self.r1 = 64 // nx
        self.t2 = -(-TAPS // ny)


def kernel(
    plan,
    mask_ref, feat_hbm, cot_hbm, w1_hbm, w2_hbm,
    fg, ag,
    feat, cot, w1, w2, wf, w1r, w2r, b1,
    pad_i, pad_g, pad_p, st_i, st_g, st_p,
    send_a, recv_a, send_b, recv_b,
    pg_t, hid_t,
    grads, r0, s1_send, s1_recv, s1_own, s2_send, s2_recv, z_all,
    load_sem, ha_sems, hb_sems, red_send, red_recv,
):
    nz, nx, ny = plan.nz, plan.nx, plan.ny
    n1, n2, r1, t2 = nx, ny, plan.r1, plan.t2
    core = lax.axis_index("dp")
    blk = lax.axis_index("blk")
    cz = blk // (nx * ny)
    cx = (blk // ny) % nx
    cy = blk % ny

    loads = [
        pltpu.make_async_copy(src, dst, load_sem.at[n])
        for n, (src, dst) in enumerate(((feat_hbm, feat), (cot_hbm, cot), (w1_hbm, w1), (w2_hbm, w2)))
    ]
    for copy in loads:
        copy.start()

    step1 = ny - (ny - 1) * core
    step2 = 1 + (ny - 1) * core
    c1 = cx + (cy - cx) * core
    c2 = cy + (cx - cy) * core
    base1 = blk - c1 * step1
    base2 = blk - c2 * step2
    plane = blk - cz * (nx * ny)

    def peer1(k):
        return (core, base1 + (c1 + k) % n1 * step1)

    def peer2(k):
        return (core, base2 + (c2 + k) % n2 * step2)

    def peerz(k):
        return (core, plane + (cz + k) % nz * (nx * ny))

    partner = (1 - core, blk)

    def valid(d):
        inside = None
        for place, count, v in ((cz, nz, d[0]), (cx, nx, d[1]), (cy, ny, d[2])):
            if v == 0:
                continue
            test = place < count - 1 if v > 0 else place > 0
            inside = test if inside is None else jnp.logical_and(inside, test)
        return inside

    inside = {d: valid(d).astype(jnp.int32) for d in DIRS}

    def target(d):
        here = inside[d]
        step = d[0] * (nx * ny) + d[1] * ny + d[2]
        return (core + (1 - here) * (1 - 2 * core), blk + here * step)

    barrier = pltpu.get_barrier_semaphore()
    peers = [target(d) for d in DIRS if sum(abs(v) for v in d) > 1]
    peers += [peerz(k) for k in range(1, nz)] + [partner]
    peers += [peer1(k) for k in range(1, n1)] + [peer2(k) for k in range(1, n2)]
    for peer in peers:
        pl.semaphore_signal(barrier, inc=1, device_id=peer, device_id_type=MESH)
    count = len(peers)

    keep = mask_ref[0, 0].astype(jnp.float32)

    def fill_own(pad, values):
        pad3 = pad.reshape((T + 2) * (T + 2), ZS, C)
        for x in range(T):
            pad3[(x + 1) * (T + 2) + 1:(x + 1) * (T + 2) + 1 + T, 8:16, :] = (
                values[x * 64:(x + 1) * 64].reshape(T, T, C)
            )

    def stage(d, pad, send, base):
        for n, (start, stride, size) in enumerate(boundary_tiles(d, False)):
            send[base + n, 0:size] = pad[rows_of(start, stride, size), :].astype(jnp.bfloat16)

    def fill_halo(d, pad, recv, base):
        for n, (start, stride, size) in enumerate(boundary_tiles(d, True)):
            tile = recv[base + n, 0:size].astype(jnp.float32)
            pad[rows_of(start, stride, size), :] = jnp.where(inside[d] > 0, tile, jnp.zeros_like(tile))

    def halo_start(send, recv, sems, arrays):
        for d in DIRS:
            here, there = OFFS[INDEX[d]] * arrays, OFFS[INDEX[opposite(d)]] * arrays
            size = SIZES[INDEX[d]] * arrays
            pltpu.make_async_remote_copy(
                src_ref=send.at[pl.ds(here, size)],
                dst_ref=recv.at[pl.ds(here + inside[d] * (there - here), size)],
                send_sem=sems.at[0], recv_sem=sems.at[1], device_id=target(d), device_id_type=MESH,
            ).start()

    def halo_all(send, recv, sems, arrays):
        return pltpu.make_async_remote_copy(
            src_ref=send, dst_ref=recv, send_sem=sems.at[0], recv_sem=sems.at[1],
            device_id=partner, device_id_type=MESH,
        )

    def halo_wait(*args):
        halo_all(*args).wait_recv()

    def halo_sent(*args):
        halo_all(*args).wait_send()

    def build(pad, stacked, reverse):
        pad3 = pad.reshape((T + 2) * (T + 2), ZS, C)

        def body(x, carry):
            for c in range(3):
                shift_z = 2 - c if reverse else c
                column = pad3[pl.ds(x * (T + 2), T + 2), 7 + shift_z:15 + shift_z, :]
                for b in range(3):
                    shift_y = 2 - b if reverse else b
                    lanes = (3 * b + c) * C
                    stacked[x, :, lanes:lanes + C] = (
                        column[shift_y:shift_y + T].reshape(64, C).astype(jnp.bfloat16)
                    )
            return carry

        lax.fori_loop(0, T + 2, body, 0)

    def slab(stacked, a):
        return stacked[a:a + T].reshape(512, K3)

    loads[0].wait()
    loads[1].wait()
    inputs = feat[...].astype(jnp.float32) * keep
    grads_out = cot[...].astype(jnp.float32) * keep
    fill_own(pad_i, inputs)
    fill_own(pad_g, grads_out)
    for d in DIRS:
        size = SIZES[INDEX[d]]
        stage(d, pad_i, send_a, OFFS[INDEX[d]] * 2)
        stage(d, pad_g, send_a, OFFS[INDEX[d]] * 2 + size)
    pl.semaphore_wait(barrier, count)
    args_a = (send_a, recv_a, ha_sems, 2)
    halo_start(*args_a)

    for g in range(2):
        grads[g, n2 - 1, :, (TAPS - (n2 - 1) * t2) * C:] = jnp.zeros((C, (n2 * t2 - TAPS) * C), jnp.float32)
    loads[2].wait()
    loads[3].wait()
    for w, arranged, stacked in ((w1, w1r, b1), (w2, w2r, None)):
        wf[...] = w[...].astype(jnp.float32)

        def arrange(n, carry):
            row = pl.multiple_of(n * 16, 16)
            for tap in range(TAPS):
                part = wf[pl.ds(n * (16 * TAPS) + tap, 16, stride=TAPS), :].astype(jnp.bfloat16)
                arranged[pl.ds(row, 16), tap * C:(tap + 1) * C] = part
                if stacked is not None:
                    stacked[pl.ds(pl.multiple_of(tap * C + n * 16, 16), 16), :] = part
            return carry

        lax.fori_loop(0, C // 16, arrange, 0)

    halo_wait(*args_a)
    for d in DIRS:
        size = SIZES[INDEX[d]]
        fill_halo(d, pad_i, recv_a, OFFS[INDEX[d]] * 2)
        fill_halo(d, pad_g, recv_a, OFFS[INDEX[d]] * 2 + size)
    build(pad_i, st_i, False)
    build(pad_g, st_g, True)

    def conv_back(stacked, weight):
        total = None
        for a in range(3):
            term = lax.dot_general(
                slab(stacked, 2 - a), weight[:, a * K3:(a + 1) * K3],
                (((1,), (1,)), ((), ())), preferred_element_type=jnp.float32,
            )
            total = term if total is None else total + term
        return total

    recv_first = dict(pair=0, s1=n2, s2=2 * n2, zs=2 * n2 + 1, a2=2 * n2 + 2, a1=3 * n2 + 1, a0=3 * n2 + n1)
    send_index = {name: n for n, name in enumerate(recv_first)}

    def remote(src, dst, g, name, n, peer):
        return pltpu.make_async_remote_copy(
            src_ref=src, dst_ref=dst,
            send_sem=red_send.at[g, send_index[name]], recv_sem=red_recv.at[g, recv_first[name] + n],
            device_id=peer, device_id_type=MESH,
        )

    def arrived(ref, g, name, n=0):
        remote(ref, ref, g, name, n, partner).wait_recv()

    def sent(ref, g, name):
        remote(ref, ref, g, name, 0, partner).wait_send()

    def go(copy):
        copy.start()

    mine = pl.multiple_of(core * 64, 64)
    other = pl.multiple_of(64 - core * 64, 64)
    firsts = ((c2, c1), (c1, c2))
    hop1 = (peer2, peer1)
    hop2 = (peer1, peer2)

    def chunk(g, i):
        own = firsts[g][1]
        return own if i == n2 - 1 else i + (i >= own).astype(jnp.int32)

    def pair_copy(g, j):
        return remote(grads.at[g, j, pl.ds(other, 64)], r0.at[g, j], g, "pair", j, partner)

    def chip(g, j, block):
        here = pl.multiple_of(block % n1 * r1, r1)
        return grads[g, j, pl.ds(mine + here, r1), :] + r0[g, j, pl.ds(here, r1), :]

    def s1_copy(g, i, k):
        return remote(s1_send.at[g, i, k - 1], s1_recv.at[g, i, k - 1], g, "s1", i, hop1[g](k))

    def s2_copy(g, i):
        k = (chunk(g, i) - firsts[g][1] + n2) % n2
        return remote(s2_send.at[g, i], s2_recv.at[g, k - 1], g, "s2", 0, hop2[g](k))

    def z_copy(g, k):
        ref = z_all.at[g, cz]
        return remote(ref, ref, g, "zs", 0, peerz(k))

    def a2_copy(g, k, wait):
        b, j = firsts[g]
        ref = ag.at[g, core, b, (j + (n2 - k)) % n2 if wait else j]
        return remote(ref, ref, g, "a2", k - 1, hop2[g](k))

    def a1_copy(g, m, k):
        b, j = firsts[g]
        ref = ag.at[g, core, b, (j + (n2 - m)) % n2]
        return remote(ref, ref, g, "a1", k - 1, hop1[g](k))

    def a0_copy(g, n, wait):
        ref = ag.at[g, 1 - core if wait else core, (firsts[g][1 if wait else 0] + (n1 - n)) % n1]
        return remote(ref, ref, g, "a0", n, partner)

    def corr(g, lhs_t, slab_of):
        sent = 0
        for a in range(3):
            part = jnp.dot(lhs_t[...], slab_of(a), preferred_element_type=jnp.float32)
            for n in range(9):
                tap = 9 * a + n
                at = tap % t2 * C
                grads[g, tap // t2, :, at:at + C] = part[:, n * C:(n + 1) * C]
            while sent < n2 and min((sent + 1) * t2, TAPS) <= 9 * (a + 1):
                go(pair_copy(g, sent))
                sent += 1

    far_first = (3, 2, 1)

    def scatter1(g):
        for i in range(n2):
            j = chunk(g, i)
            pair_copy(g, j).wait_recv()
            for k in far_first:
                s1_send[g, i, k - 1] = chip(g, j, firsts[g][0] + k).astype(jnp.bfloat16)
                go(s1_copy(g, i, k))

    def scatter2(g):
        for i in range(n2):
            total = chip(g, chunk(g, i), firsts[g][0])
            arrived(s1_recv.at[g, i], g, "s1", i)
            for k in range(1, n1):
                total = total + s1_recv[g, i, k - 1].astype(jnp.float32)
            if i < n2 - 1:
                s2_send[g, i] = total.astype(jnp.bfloat16)
                go(s2_copy(g, i))
            else:
                s1_own[g] = total

    z_order = (4, 3, 5, 2, 6, 1, 7)

    def scatter3(g):
        total = s1_own[g]
        arrived(s2_recv.at[g], g, "s2")
        for k in range(1, n2):
            total = total + s2_recv[g, k - 1].astype(jnp.float32)
        z_all[g, cz] = total.astype(jnp.bfloat16)
        for k in z_order:
            go(z_copy(g, k))

    def gather2(g):
        arrived(z_all.at[g, pl.ds(0, nz - 1)], g, "zs")
        total = z_all[g, 0].astype(jnp.float32)
        for z in range(1, nz):
            total = total + z_all[g, z].astype(jnp.float32)
        b, j = firsts[g]
        ag[g, core, b, j] = (total * UNSCALE).astype(jnp.bfloat16)
        for k in far_first:
            go(a2_copy(g, k, False))
        for k in far_first:
            go(a1_copy(g, 0, k))

    def gather1(g):
        for m in (3, 1, 2):
            a2_copy(g, m, True).wait_recv()
            for k in far_first:
                go(a1_copy(g, m, k))
        go(a0_copy(g, 0, False))

    def gather0(g):
        for k in (3, 1, 2):
            block = (firsts[g][0] + (n1 - k)) % n1
            arrived(ag.at[g, core, block], g, "a1", k - 1)
            go(a0_copy(g, k, False))

    def finish(g):
        for n in (0, 3, 1, 2):
            a0_copy(g, n, True).wait_recv()

    pre_act = None
    for a in range(3):
        term = jnp.dot(slab(st_i, a), b1[a * K3:(a + 1) * K3, :], preferred_element_type=jnp.float32)
        pre_act = term if pre_act is None else pre_act + term
    sigma = 1.0 / (1.0 + jnp.exp(-pre_act))
    hid_t[...] = (pre_act * sigma * keep).T.astype(jnp.bfloat16)
    corr(0, hid_t, lambda a: slab(st_g, 2 - a))
    back = conv_back(st_g, w2r)
    pre_grad = back * sigma * (1.0 + pre_act * (1.0 - sigma)) * keep
    fill_own(pad_p, pre_grad)
    pg_t[...] = pre_grad.T.astype(jnp.bfloat16)
    scatter1(0)
    corr(1, pg_t, lambda a: slab(st_i, a))
    for d in DIRS:
        stage(d, pad_p, send_b, OFFS[INDEX[d]])
    scatter1(1)
    args_b = (send_b, recv_b, hb_sems, 1)
    halo_start(*args_b)
    scatter2(0)
    scatter2(1)
    scatter3(0)
    halo_wait(*args_b)
    for d in DIRS:
        fill_halo(d, pad_p, recv_b, OFFS[INDEX[d]])
    build(pad_p, st_p, True)
    scatter3(1)
    result = conv_back(st_p, w1r)
    fg[...] = ((cot[...].astype(jnp.float32) * keep + result) * keep).astype(jnp.bfloat16)
    gather2(0)
    gather2(1)
    gather1(0)
    gather1(1)
    gather0(0)
    gather0(1)
    finish(0)
    finish(1)

    halo_sent(*args_a)
    halo_sent(*args_b)
    for g in range(2):
        sent(r0.at[g], g, "pair")
        sent(s1_send.at[g], g, "s1")
        sent(s2_send.at[g], g, "s2")
        sent(z_all.at[g, pl.ds(0, nz - 1)], g, "zs")
        sent(s1_send.at[g, 0], g, "a2")
        sent(s1_send.at[g], g, "a1")
        sent(ag.at[g, core], g, "a0")


def unpack_kernel(plan, ag, fg, g1_hbm, g2_hbm, fg_out, g1, g2, store_sem):
    n1, r1, t2 = plan.nx, plan.r1, plan.t2
    rows = r1 * TAPS
    blocks = [(half, block) for half in range(2) for block in range(n1)]

    store_fg = pltpu.make_async_copy(fg, fg_out, store_sem.at[2])
    store_fg.start()
    for half, block in blocks:
        first = (half * n1 + block) * rows
        for tap in range(TAPS):
            g2[pl.ds(first + tap, r1, stride=TAPS), :] = (
                ag[0, half, block, tap // t2, :, pl.ds(tap % t2 * C, C)].astype(jnp.float32)
            )
        pltpu.make_async_copy(g2.at[pl.ds(first, rows)], g2_hbm.at[pl.ds(first, rows)], store_sem.at[0]).start()
    for tap in range(TAPS):
        square = ag[1, :, :, tap // t2, :, pl.ds(tap % t2 * C, C)].reshape(C, C)
        g1[pl.ds(tap, C, stride=TAPS), :] = square.astype(jnp.float32).T
    for n in range(2 * n1):
        part = pl.ds(n * rows, rows)
        pltpu.make_async_copy(g1.at[part], g1_hbm.at[part], store_sem.at[1]).start()
    pltpu.make_async_copy(g2, g2_hbm, store_sem.at[0]).wait()
    pltpu.make_async_copy(g1, g1_hbm, store_sem.at[1]).wait()
    store_fg.wait()


def on_device(plan, features, tile_mask, w_first, w_second, cotangent):
    n1, n2, nz, r1, t2 = plan.nx, plan.ny, plan.nz, plan.r1, plan.t2
    f32, bf16 = jnp.float32, jnp.bfloat16
    rows = TAPS * C
    gathered = (2, 2, n1, n2, r1, t2 * C)
    s1_buf = pltpu.VMEM((2, n2, n1 - 1, r1, t2 * C), bf16)
    s2_buf = pltpu.VMEM((2, n2 - 1, r1, t2 * C), bf16)
    pad = pltpu.VMEM(((T + 2) * (T + 2) * ZS, C), f32)
    stacked = pltpu.VMEM((T + 2, 64, K3), bf16)
    halo_a = pltpu.VMEM((2 * TILES, 8, C), bf16)
    halo_b = pltpu.VMEM((TILES, 8, C), bf16)
    dma = pltpu.SemaphoreType.DMA
    vmem_spec = pl.BlockSpec(memory_space=pltpu.VMEM)
    any_spec = pl.BlockSpec(memory_space=pl.ANY)
    scratch = [
        pltpu.VMEM((512, C), bf16), pltpu.VMEM((512, C), bf16),
        pltpu.VMEM((rows, C), bf16), pltpu.VMEM((rows, C), bf16), pltpu.VMEM((rows, C), f32),
        pltpu.VMEM((C, rows), bf16), pltpu.VMEM((C, rows), bf16), pltpu.VMEM((rows, C), bf16),
        pad, pad, pad, stacked, stacked, stacked,
        halo_a, halo_a, halo_b, halo_b,
        pltpu.VMEM((C, 512), bf16), pltpu.VMEM((C, 512), bf16),
        pltpu.VMEM((2, n2, C, t2 * C), f32), pltpu.VMEM((2, n2, 64, t2 * C), f32),
        s1_buf, s1_buf, pltpu.VMEM((2, r1, t2 * C), f32), s2_buf, s2_buf,
        pltpu.VMEM((2, nz, r1, t2 * C), bf16),
        dma((4,)), dma((2,)), dma((2,)), dma((2, 7)), dma((2, 3 * n2 + 2 * n1)),
    ]
    partial_fg, partial_ag = pl.pallas_call(
        functools.partial(kernel, plan),
        out_shape=(pltpu.VMEM((512, C), bf16), pltpu.VMEM(gathered, bf16)),
        in_specs=[pl.BlockSpec(memory_space=pltpu.SMEM)] + [any_spec] * 4,
        out_specs=(vmem_spec,) * 2,
        scratch_shapes=scratch,
        compiler_params=pltpu.CompilerParams(
            collective_id=0, has_side_effects=True, vmem_limit_bytes=56 * 1024 * 1024
        ),
        name="block_backward",
    )(tile_mask, features[0], cotangent[0], w_first, w_second)
    grad_first, grad_second, feature_grad = pl.pallas_call(
        functools.partial(unpack_kernel, plan),
        out_shape=(
            jax.ShapeDtypeStruct((rows, C), f32),
            jax.ShapeDtypeStruct((rows, C), f32),
            jax.ShapeDtypeStruct((512, C), bf16),
        ),
        in_specs=[vmem_spec] * 2,
        out_specs=(any_spec,) * 3,
        scratch_shapes=[
            pltpu.VMEM((rows, C), f32), pltpu.VMEM((rows, C), f32), dma((3,)),
        ],
        compiler_params=pltpu.CompilerParams(vmem_limit_bytes=16 * 1024 * 1024),
        name="unpack",
    )(partial_ag, partial_fg)
    return grad_first, grad_second, feature_grad[None]


def solution(mesh):
    blocks = mesh.shape["blk"]
    ny = nx = 4 if blocks >= 16 else 2
    plan = Plan(blocks // (nx * ny), nx, ny)
    in_specs = (P("dp", "blk", None), P("dp", "blk"), P(), P(), P("dp", "blk", None))
    out_specs = (P(), P(), P("dp", "blk", None))
    return jax.shard_map(
        functools.partial(on_device, plan), mesh=mesh, in_specs=in_specs, out_specs=out_specs, check_vma=False
    )
```
